256 devices in a mesh: blk: 16 (over z, x_hi), grp: 16 (over y, x_lo, core).
Axes of the slice: x: 4 (x_hi: 2, x_lo: 2; x = x_hi * 2 + x_lo), y: 4, z: 8, core: 2. Of those that a mesh axis runs over, the one named last changes fastest.
Arguments:
- coil_pos: float32 [3, 10240], P(None, ('blk', 'grp')), may hold values from -1 to 1
- coil_radius: float32 [10240], P(('blk', 'grp')), may hold values from 0.02 to 0.08
- coil_current: bfloat16 [64, 10240], P(None, ('blk', 'grp')), may hold values from -0.109375 to 0.109375
- blank_pos: float32 [3, 32768], P(None, ('blk', 'grp')), may hold values from -1 to 1
- blank_rule: int32 [32768], P(('blk', 'grp')), may hold values from 0 to 7
- blank_cond: float32 [32768], P(('blk', 'grp')), may hold values from 0.3 to 3
- quad_offset: float32 [3, 8, 2], replicated, may hold values from -0.1 to 0.1
- quad_weight: float32 [8, 2], replicated, may hold values from 0.3 to 0.7
Outputs:
- blank_current: bfloat16 [64, 32768], P(None, ('blk', 'grp'))
- coil_reaction: float32 [64, 10240], P(None, ('blk', 'grp'))
The draws below stay inside these ranges and needn't reach their ends.
All inputs are finite; a program needn't handle non-finite values.
Results may differ from the reference program's by a relative error of at most 0.0066.
Values may be sent and summed in bfloat16 or wider, within the bound.
No kernel may reach another device: no remote copies, remote signals or barrier semaphores. Data moves between devices by JAX's collectives and lax.ppermute only.
A program may use at most 64 MiB of HBM per device.

```python
import math
import jax
import jax.numpy as jnp
from jax import lax

COIL_DEV = 40
SAMPLES = 64
QUAD = 2
RULES = 8
COILS = 10240
BLANKS = 32768


def plant(result, rng, least, top_value):
    spot = [jax.random.randint(jax.random.fold_in(rng, axis), (), 0, length) for axis, length in enumerate(result.shape)]
    widest = result.shape.index(max(result.shape))
    next_to = spot[:widest] + [(spot[widest] + 1) % result.shape[widest]] + spot[widest + 1:]
    return result.at[tuple(spot)].set(least).at[tuple(next_to)].set(top_value)


def block_scale(key, shape, pieces, low, high):
    loudness = 1.0
    for axis_at, shards_of in pieces:
        steps = jax.random.uniform(jax.random.fold_in(jax.random.fold_in(key, 6), axis_at), (shards_of,), jnp.float32, low / len(pieces), high / len(pieces))
        loudness = loudness * jnp.repeat(jnp.exp(steps), shape[axis_at] // shards_of).reshape((-1,) + (1,) * (len(shape) - 1 - axis_at))
    return loudness


def centred(rng, extent, spread, limit, shards=(), kind=jnp.bfloat16):
    result = jax.random.normal(rng, extent, jnp.float32) * spread
    if len(shards) > 0:
        result = block_scale(rng, extent, shards, -0.22, 0.18) * result
    return jnp.clip(result, min=-limit, max=limit).astype(kind)


def setup_inputs(seed: int = 0) -> dict:
    key_list = jax.random.split(jax.random.key(seed), 9)
    return {
        "coil_pos": jnp.clip(jax.random.uniform(key_list[0], (3, COILS), jnp.float32, -1.0, 1.0) * block_scale(key_list[0], (3, COILS), ((1, 256),), -0.4, 0.0), -1.0, 1.0),
        "coil_radius": jnp.clip(jnp.exp(math.log(0.08) - 1.3862944 * jax.random.uniform(key_list[1], (COILS,), jnp.float32) ** block_scale(key_list[1], (COILS,), ((0, 256),), -0.2, 0.2)), 0.02, 0.08),
        "coil_current": centred(key_list[2], (SAMPLES, COILS), (0.7 / COILS ** 0.5), 0.109375, ((1, 256),)),
        "blank_pos": jnp.clip(jax.random.uniform(key_list[3], (3, BLANKS), jnp.float32, -1.0, 1.0) * block_scale(key_list[3], (3, BLANKS), ((1, 256),), -0.4, 0.0), -1.0, 1.0),
        "blank_rule": plant(jax.random.randint(key_list[4], (BLANKS,), 0, RULES), jax.random.fold_in(key_list[4], 1), 0, RULES - 1).astype(jnp.int32),
        "blank_cond": jnp.clip(jnp.exp(math.log(3.0) - 2.3025851 * jax.random.uniform(key_list[5], (BLANKS,), jnp.float32) ** block_scale(key_list[5], (BLANKS,), ((0, 256),), -0.2, 0.2)), 0.3, 3.0),
        "quad_offset": jnp.clip(jax.random.uniform(key_list[6], (3, RULES, QUAD), jnp.float32, -0.1, 0.1), -0.1, 0.1),
        "quad_weight": jnp.clip(jax.random.uniform(key_list[7], (RULES, QUAD), jnp.float32, 0.3, 0.7), 0.3, 0.7),
    }


def blank_geometry(blank_pos, blank_rule, quad_offset, quad_weight):
    rules = quad_weight.shape[0]
    points = quad_weight.shape[1]
    onehot = (blank_rule[None, :] == jnp.arange(rules, dtype=jnp.int32)[:, None]).astype(jnp.float32)
    table_rows = []
    base_rows = []
    zeros_row = jnp.zeros_like(blank_pos[0])
    for point in range(points):
        table_rows += [quad_offset[0, :, point], quad_offset[1, :, point], quad_offset[2, :, point], quad_weight[:, point]]
        base_rows += [blank_pos[0], blank_pos[1], blank_pos[2], zeros_row]
    table = jnp.stack(table_rows, 0)
    base = jnp.stack(base_rows, 0)
    return base + jnp.dot(table, onehot, precision=lax.Precision.HIGHEST)

def kernel_block(coil_geometry, geometry):
    points = geometry.shape[0] // 4
    running = jnp.zeros((coil_geometry.shape[1], geometry.shape[1]), jnp.float32)
    for point in range(points):
        delta_x = coil_geometry[0][:, None] - geometry[4 * point][None, :]
        delta_y = coil_geometry[1][:, None] - geometry[4 * point + 1][None, :]
        delta_z = coil_geometry[2][:, None] - geometry[4 * point + 2][None, :]
        squared = delta_x * delta_x + delta_y * delta_y + delta_z * delta_z + coil_geometry[3][:, None]
        running = running + geometry[4 * point + 3][None, :] * lax.rsqrt(squared)
    return running

def reference(coil_pos, coil_radius, coil_current, blank_pos, blank_rule, blank_cond, quad_offset, quad_weight):
    coil_geometry = jnp.concatenate([coil_pos, (coil_radius * coil_radius)[None, :]], 0)
    geometry = blank_geometry(blank_pos, blank_rule, quad_offset, quad_weight)
    groups = COILS // COIL_DEV
    grouped_geometry = coil_geometry.reshape(4, groups, COIL_DEV).transpose(1, 0, 2)
    grouped_current = coil_current.reshape(SAMPLES, groups, COIL_DEV).transpose(1, 0, 2)

    def first_pass(running, inputs):
        group_geometry, group_current = inputs
        kernel_tile = kernel_block(group_geometry, geometry).astype(jnp.bfloat16)
        return (running + jnp.dot(group_current, kernel_tile, preferred_element_type=jnp.float32), None)
    induced, _ = lax.scan(first_pass, jnp.zeros((SAMPLES, BLANKS), jnp.float32), (grouped_geometry, grouped_current))
    blank_current = induced.astype(jnp.bfloat16)
    weighted = (blank_cond[None, :] * blank_current.astype(jnp.float32)).astype(jnp.bfloat16)

    def second_pass(carried, group_geometry):
        kernel_tile = kernel_block(group_geometry, geometry).astype(jnp.bfloat16)
        product = lax.dot_general(weighted, kernel_tile, (((1,), (1,)), ((), ())), preferred_element_type=jnp.float32)
        return (carried, product)
    _, portions = lax.scan(second_pass, jnp.zeros((), jnp.float32), grouped_geometry)
    coil_reaction = portions.transpose(1, 0, 2).reshape(SAMPLES, COILS) * (2.0 / BLANKS)
    return (blank_current, coil_reaction)
```

```python
import jax
import jax.numpy as jnp
from jax import lax
from jax.experimental import pallas as pl
from jax.experimental.pallas import tpu as pltpu
from jax.sharding import Mesh
from jax.sharding import PartitionSpec as P

AXES = ("zh", "zl", "xh", "y", "xl", "core")
SIZES = (4, 2, 2, 4, 2, 2)
ROWS = ("zh",)
COLS = ("zl", "xh", "y", "xl")
LANES = 128
BF16 = jnp.bfloat16
F32 = jnp.float32


def parts_of(value):
    high = value.astype(BF16).astype(F32)
    rest = value - high
    mid = rest.astype(BF16).astype(F32)
    low = (rest - mid).astype(BF16).astype(F32)
    return [high, mid, low]


def prepare(pos_ref, radius_ref, current_ref, blank_ref, rule_ref, cond_ref, payload_ref, tile_ref):
    samples = current_ref.shape[1]
    coils = current_ref.shape[0]
    x, y, z = (pos_ref[pl.ds(axis, 1), :] for axis in range(3))
    radius = radius_ref[...]
    square = x * x + y * y + z * z + radius * radius
    rows = []
    for value in (x, y, z):
        for part in parts_of(value):
            rows += [part, part, part]
    rows += parts_of(square)
    rows += [jnp.ones_like(x)] * 3
    rows.append(jnp.zeros((LANES - samples - len(rows), coils), F32))
    geometry = jnp.concatenate(rows, 0).T
    payload = jnp.concatenate([current_ref[...].astype(F32), geometry], 1).astype(BF16)
    for copy in range(payload_ref.shape[0]):
        payload_ref[copy] = payload
    rule = rule_ref[...].astype(F32)
    tile_ref[...] = jnp.concatenate(
        [blank_ref[...], rule, cond_ref[...], jnp.zeros((3, rule.shape[1]), F32)], 0
    )


def blank_features(samples, offset_ref, weight_ref, *refs):
    tiles, (feature_ref, row_ref) = refs[:-2], refs[-2:]
    rules, points = weight_ref.shape
    base = [jnp.concatenate([tile[pl.ds(row, 1), :] for tile in tiles], 1) for row in range(5)]
    rule, cond = base[3], base[4]
    weights = []
    for point in range(points):
        place = []
        offsets = [jnp.zeros_like(rule) for _ in range(3)]
        weight = jnp.zeros_like(rule)
        for number in range(rules):
            here = rule == float(number)
            for axis in range(3):
                offsets[axis] = jnp.where(here, offset_ref[axis, number, point], offsets[axis])
            weight = jnp.where(here, weight_ref[number, point], weight)
        weights.append(weight)
        place = [base[axis] + offsets[axis] for axis in range(3)]
        square = place[0] * place[0] + place[1] * place[1] + place[2] * place[2]
        rows = [jnp.zeros((samples, rule.shape[1]), F32)]
        for value in place:
            rows += [-2.0 * part for part in parts_of(value)] * 3
        rows += [jnp.ones_like(rule)] * 3
        rows += parts_of(square)
        filled = sum(row.shape[0] for row in rows)
        rows.append(jnp.zeros((LANES - filled, rule.shape[1]), F32))
        feature_ref[point] = jnp.concatenate(rows, 0).astype(BF16)
    row_ref[...] = jnp.concatenate([*weights, cond, jnp.zeros((5, rule.shape[1]), F32)], 0)


def form(first, tile, payload_ref, feature_ref, row_ref, *refs):
    if first:
        kernel_ref, out_ref = refs
    else:
        before_ref, kernel_ref, out_ref = refs
    samples = out_ref.shape[0]
    points = feature_ref.shape[0]
    total = None
    for step in range(payload_ref.shape[0] // tile):
        at = pl.ds(step * tile, tile)
        payload = payload_ref[at, :]
        block = None
        for point in range(points):
            squared = jnp.dot(payload, feature_ref[point], preferred_element_type=F32)
            term = row_ref[pl.ds(point, 1), :] * lax.rsqrt(squared)
            block = term if block is None else block + term
        block = block.astype(BF16)
        kernel_ref[at, :] = block
        product = lax.dot_general(
            payload, block, (((0,), (0,)), ((), ())), preferred_element_type=F32
        )
        total = product if total is None else total + product
    total = total[:samples]
    if not first:
        total = total + before_ref[...]
    out_ref[...] = total.astype(out_ref.dtype)


def react(row_ref, *refs):
    arrivals = refs[:-6]
    own_kernel_ref, other_kernel_ref, current_ref, weighted_ref, own_ref, other_ref = refs[-6:]
    count = len(arrivals)
    width = current_ref.shape[1]
    blocks = []
    for block in range(count):
        total = None
        for behind in range(count):
            piece = arrivals[behind][:, pl.ds((block - behind) % count * width, width)].astype(F32)
            total = piece if total is None else total + piece
        blocks.append(total.astype(BF16))
    current_ref[...] = blocks[0]
    current = jnp.concatenate(blocks, 1).astype(F32)
    weighted = (row_ref[pl.ds(2, 1), :] * current).astype(BF16)
    weighted_ref[...] = weighted
    for kernel_ref, out_ref in ((other_kernel_ref, other_ref), (own_kernel_ref, own_ref)):
        out_ref[...] = lax.dot_general(
            kernel_ref[...], weighted, (((1,), (1,)), ((), ())), preferred_element_type=F32
        ).astype(out_ref.dtype)


def from_behind(value, axis, by):
    size = lax.axis_size(axis)
    return lax.ppermute(value, axis, [(i, (i + by) % size) for i in range(size)])


def shaped(shape, dtype):
    return jax.ShapeDtypeStruct(shape, dtype)


def per_device(
    coil_pos, coil_radius, coil_current, blank_pos, blank_rule, blank_cond, quad_offset, quad_weight
):
    samples, coils = coil_current.shape
    blanks = blank_pos.shape[1]
    total_blanks = blanks * lax.axis_size(AXES)
    cols = lax.axis_size(COLS)
    rows = lax.axis_size(ROWS)
    points = quad_weight.shape[1]
    held = cols * coils
    width = rows * blanks

    payload, tile = pl.pallas_call(
        prepare,
        out_shape=(shaped((cols, coils, LANES), BF16), shaped((8, blanks), F32)),
        name="prepare",
    )(
        coil_pos,
        coil_radius[None, :],
        coil_current.T,
        blank_pos,
        blank_rule[None, :],
        blank_cond[None, :],
    )
    own = lax.all_to_all(payload, COLS, 0, 0, tiled=True).reshape(held, LANES)
    tiles = [tile] + [from_behind(tile, ROWS, by) for by in range(1, rows)]
    smem = pl.BlockSpec(memory_space=pltpu.SMEM)
    vmem = pl.BlockSpec(memory_space=pltpu.VMEM)
    features, table = pl.pallas_call(
        lambda *refs: blank_features(samples, *refs),
        out_shape=(shaped((points, LANES, width), BF16), shaped((8, width), F32)),
        in_specs=[smem, smem] + [vmem] * rows,
        name="blank_features",
    )(quad_offset, quad_weight, *tiles)

    other = from_behind(own, "core", 1)
    cost = pl.CostEstimate(
        flops=2 * held * width * LANES * (points + 1),
        transcendentals=points * held * width,
        bytes_accessed=2 * held * (width + LANES),
    )
    step = 256 if held % 256 == 0 else held
    own_kernel, partial = pl.pallas_call(
        lambda *refs: form(True, step, *refs),
        out_shape=(shaped((held, width), BF16), shaped((samples, width), F32)),
        cost_estimate=cost,
        name="form_own",
    )(own, features, table)
    other_kernel, partial = pl.pallas_call(
        lambda *refs: form(False, step, *refs),
        out_shape=(shaped((held, width), BF16), shaped((samples, width), BF16)),
        cost_estimate=cost,
        name="form_other",
    )(other, features, table, partial)

    arrivals = [partial] + [from_behind(partial, ROWS, by) for by in range(1, rows)]
    blank_current, _, own_reaction, other_reaction = pl.pallas_call(
        react,
        out_shape=(
            shaped((samples, blanks), BF16),
            shaped((samples, width), BF16),
            shaped((held, samples), F32),
            shaped((held, samples), BF16),
        ),
        name="react",
    )(table, *arrivals, own_kernel, other_kernel)
    reaction = own_reaction + from_behind(other_reaction, "core", 1).astype(F32)
    pieces = reaction.astype(BF16).reshape(cols, coils, samples)
    arrived = lax.all_to_all(pieces, COLS, 0, 0, tiled=True)
    summed = arrived.astype(F32).sum(axis=0) * (2.0 / total_blanks)
    return (blank_current, summed.T)


def solution(mesh):
    split = Mesh(mesh.devices.reshape(SIZES), AXES)
    whole = P(None, AXES)
    return jax.shard_map(
        per_device,
        mesh=split,
        in_specs=(whole, P(AXES), whole, whole, P(AXES), P(AXES), P(), P()),
        out_specs=(whole, whole),
        check_vma=False,
    )
```

```python
import jax
import jax.numpy as jnp
from jax import lax
from jax.experimental import pallas as pl
from jax.experimental.pallas import tpu as pltpu
from jax.sharding import Mesh
from jax.sharding import PartitionSpec as P

AXES = ("zh", "zl", "xh", "y", "xl", "core")
SIZES = (4, 2, 2, 4, 2, 2)
ROWS = ("zh",)
COLS = ("zl", "xh", "y", "xl")
LANES = 128
BF16 = jnp.bfloat16
F32 = jnp.float32
ROOM = pltpu.CompilerParams(vmem_limit_bytes=16 << 20)


def parts_of(value):
    high = value.astype(BF16).astype(F32)
    rest = value - high
    mid = rest.astype(BF16).astype(F32)
    low = (rest - mid).astype(BF16).astype(F32)
    return [high, mid, low]


def prepare(pos_ref, radius_ref, current_ref, blank_ref, rule_ref, cond_ref, payload_ref, tile_ref):
    samples = current_ref.shape[1]
    coils = current_ref.shape[0]
    x, y, z = (pos_ref[pl.ds(axis, 1), :] for axis in range(3))
    radius = radius_ref[...]
    square = x * x + y * y + z * z + radius * radius
    rows = []
    for value in (x, y, z):
        for part in parts_of(value):
            rows += [part, part, part]
    rows += parts_of(square)
    rows += [jnp.ones_like(x)] * 3
    rows.append(jnp.zeros((LANES - samples - len(rows), coils), F32))
    geometry = jnp.concatenate(rows, 0).T
    payload = jnp.concatenate([current_ref[...].astype(F32), geometry], 1).astype(BF16)
    for copy in range(payload_ref.shape[0]):
        payload_ref[copy] = payload
    rule = rule_ref[...].astype(F32)
    tile_ref[...] = jnp.concatenate(
        [blank_ref[...], rule, cond_ref[...], jnp.zeros((3, rule.shape[1]), F32)], 0
    )


def blank_features(samples, offset_ref, weight_ref, *refs):
    tiles, (feature_ref, row_ref) = refs[:-2], refs[-2:]
    points, rules = weight_ref.shape
    base = [jnp.concatenate([tile[pl.ds(row, 1), :] for tile in tiles], 1) for row in range(5)]
    rule, cond = base[3], base[4]
    weights = []
    for point in range(points):
        place = []
        offsets = [jnp.zeros_like(rule) for _ in range(3)]
        weight = jnp.zeros_like(rule)
        for number in range(rules):
            here = rule == float(number)
            for axis in range(3):
                offsets[axis] = jnp.where(here, offset_ref[axis, point, number], offsets[axis])
            weight = jnp.where(here, weight_ref[point, number], weight)
        weights.append(weight)
        place = [base[axis] + offsets[axis] for axis in range(3)]
        square = place[0] * place[0] + place[1] * place[1] + place[2] * place[2]
        rows = [jnp.zeros((samples, rule.shape[1]), F32)]
        for value in place:
            rows += [-2.0 * part for part in parts_of(value)] * 3
        rows += [jnp.ones_like(rule)] * 3
        rows += parts_of(square)
        filled = sum(row.shape[0] for row in rows)
        rows.append(jnp.zeros((LANES - filled, rule.shape[1]), F32))
        feature_ref[point] = jnp.concatenate(rows, 0).astype(BF16)
    row_ref[...] = jnp.concatenate([*weights, cond, jnp.zeros((5, rule.shape[1]), F32)], 0)


def form(first, tile, payload_ref, feature_ref, row_ref, *refs):
    if first:
        kernel_ref, out_ref = refs
    else:
        before_ref, kernel_ref, out_ref = refs
    samples = out_ref.shape[0]
    points = feature_ref.shape[0]
    total = None
    for step in range(payload_ref.shape[0] // tile):
        at = pl.ds(step * tile, tile)
        payload = payload_ref[at, :]
        block = None
        for point in range(points):
            squared = jnp.dot(payload, feature_ref[point], preferred_element_type=F32)
            term = row_ref[pl.ds(point, 1), :] * lax.rsqrt(squared)
            block = term if block is None else block + term
        block = block.astype(BF16)
        kernel_ref[at, :] = block
        product = lax.dot_general(
            payload, block, (((0,), (0,)), ((), ())), preferred_element_type=F32
        )
        total = product if total is None else total + product
    total = total[:samples]
    if not first:
        total = total + before_ref[...]
    out_ref[...] = total.astype(out_ref.dtype)


def weigh(scale, row_ref, *refs):
    arrivals = refs[:-4]
    kernel_ref, current_ref, weighted_ref, out_ref = refs[-4:]
    count = len(arrivals)
    width = current_ref.shape[1]
    blocks = []
    for block in range(count):
        total = None
        for behind in range(count):
            piece = arrivals[behind][:, pl.ds((block - behind) % count * width, width)].astype(F32)
            total = piece if total is None else total + piece
        blocks.append(total.astype(BF16))
    current_ref[...] = blocks[0]
    current = jnp.concatenate(blocks, 1).astype(F32)
    weighted = (row_ref[pl.ds(2, 1), :] * current).astype(BF16)
    weighted_ref[...] = weighted
    out_ref[...] = (scale * contract(kernel_ref[...], weighted)).astype(out_ref.dtype)


def contract(kernel, weighted):
    return lax.dot_general(kernel, weighted, (((1,), (1,)), ((), ())), preferred_element_type=F32)


def react(scale, weighted_ref, kernel_ref, out_ref):
    out_ref[...] = scale * contract(kernel_ref[...], weighted_ref[...])


def from_behind(value, axis, by):
    size = lax.axis_size(axis)
    return lax.ppermute(value, axis, [(i, (i + by) % size) for i in range(size)])


def shaped(shape, dtype):
    return jax.ShapeDtypeStruct(shape, dtype)


def per_device(
    coil_pos, coil_radius, coil_current, blank_pos, blank_rule, blank_cond, quad_offset, quad_weight
):
    samples, coils = coil_current.shape
    blanks = blank_pos.shape[1]
    total_blanks = blanks * lax.axis_size(AXES)
    cols = lax.axis_size(COLS)
    rows = lax.axis_size(ROWS)
    points = quad_weight.shape[1]
    held = cols * coils
    width = rows * blanks

    payload, tile = pl.pallas_call(
        prepare,
        out_shape=(shaped((cols, coils, LANES), BF16), shaped((8, blanks), F32)),
        name="prepare",
    )(
        coil_pos,
        coil_radius[None, :],
        coil_current.T,
        blank_pos,
        blank_rule[None, :],
        blank_cond[None, :],
    )
    own = lax.all_to_all(payload, COLS, 0, 0, tiled=True).reshape(held, LANES)
    tiles = [tile] + [from_behind(tile, ROWS, by) for by in range(1, rows)]
    smem = pl.BlockSpec(memory_space=pltpu.SMEM)
    vmem = pl.BlockSpec(memory_space=pltpu.VMEM)
    features, table = pl.pallas_call(
        lambda *refs: blank_features(samples, *refs),
        out_shape=(shaped((points, LANES, width), BF16), shaped((8, width), F32)),
        in_specs=[smem, smem] + [vmem] * rows,
        compiler_params=ROOM,
        name="blank_features",
    )(quad_offset.transpose(0, 2, 1), quad_weight.T, *tiles)
    own, features, table = lax.optimization_barrier((own, features, table))

    other = from_behind(own, "core", 1)
    cost = pl.CostEstimate(
        flops=2 * held * width * LANES * (points + 1),
        transcendentals=points * held * width,
        bytes_accessed=2 * held * (width + LANES),
    )
    step = 256 if held % 256 == 0 else held
    own_kernel, partial = pl.pallas_call(
        lambda *refs: form(True, step, *refs),
        out_shape=(shaped((held, width), BF16), shaped((samples, width), F32)),
        compiler_params=ROOM,
        cost_estimate=cost,
        name="form_own",
    )(own, features, table)
    other_kernel, partial = pl.pallas_call(
        lambda *refs: form(False, step, *refs),
        out_shape=(shaped((held, width), BF16), shaped((samples, width), BF16)),
        compiler_params=ROOM,
        cost_estimate=cost,
        name="form_other",
    )(other, features, table, partial)

    arrivals = [partial] + [from_behind(partial, ROWS, by) for by in range(1, rows)]
    scale = 2.0 / total_blanks
    react_cost = pl.CostEstimate(
        flops=2 * held * width * samples,
        transcendentals=0,
        bytes_accessed=2 * held * (width + 2 * samples),
    )
    blank_current, weighted, reaction = pl.pallas_call(
        lambda *refs: weigh(scale, *refs),
        out_shape=(
            shaped((samples, blanks), BF16),
            shaped((samples, width), BF16),
            shaped((held, samples), BF16),
        ),
        compiler_params=ROOM,
        cost_estimate=react_cost,
        name="weigh",
    )(table, *arrivals, other_kernel)
    crossed = from_behind(reaction, "core", 1)
    reaction = pl.pallas_call(
        lambda *refs: react(scale, *refs),
        out_shape=shaped((held, samples), F32),
        compiler_params=ROOM,
        cost_estimate=react_cost,
        name="react",
    )(weighted, own_kernel)
    reaction = reaction + crossed.astype(F32)
    pieces = reaction.astype(BF16).reshape(cols, coils, samples)
    arrived = lax.all_to_all(pieces, COLS, 0, 0, tiled=True)
    summed = arrived.astype(F32).sum(axis=0)
    return (blank_current, summed.T)


def solution(mesh):
    split = Mesh(mesh.devices.reshape(SIZES), AXES)
    whole = P(None, AXES)
    return jax.shard_map(
        per_device,
        mesh=split,
        in_specs=(whole, P(AXES), whole, whole, P(AXES), P(AXES), P(), P()),
        out_specs=(whole, whole),
        check_vma=False,
    )
```

```python
import jax
import jax.numpy as jnp
from jax import lax
from jax.experimental import pallas as pl
from jax.experimental.pallas import tpu as pltpu
from jax.sharding import Mesh
from jax.sharding import PartitionSpec as P

AXES = ("zh", "zl", "xh", "y", "xl", "core")
SIZES = (4, 2, 2, 4, 2, 2)
ROWS = ("y",)
COLS = ("zh", "zl", "xh", "xl")
LANES = 128
SUBLANES = 8
SLOT = 32
BF16 = jnp.bfloat16
F32 = jnp.float32
ROOM = pltpu.CompilerParams(vmem_limit_bytes=16 << 20)


def parts_of(value):
    high = value.astype(BF16).astype(F32)
    rest = value - high
    mid = rest.astype(BF16).astype(F32)
    low = (rest - mid).astype(BF16).astype(F32)
    return [high, mid, low]


def prepare(
    offset_ref,
    weight_ref,
    pos_ref,
    radius_ref,
    current_ref,
    blank_ref,
    rule_ref,
    cond_ref,
    payload_ref,
    tile_ref,
):
    coils, samples = current_ref.shape
    groups = coils // SUBLANES
    x, y, z = (pos_ref[pl.ds(axis, 1), :] for axis in range(3))
    radius = radius_ref[...]
    square = x * x + y * y + z * z + radius * radius
    rows = [part for value in (x, y, z, square) for part in parts_of(value)]
    count = len(rows)
    rows.append(jnp.zeros((16 - count, coils), F32))
    columns = jnp.concatenate(rows, 0).T
    geometry = [columns[SUBLANES * g : SUBLANES * (g + 1), :count] for g in range(groups)]
    geometry.append(jnp.zeros((SUBLANES, samples - count * groups), F32))
    geometry = jnp.concatenate(geometry, 1)
    current = current_ref[...].astype(F32)
    half = payload_ref.shape[1]
    left = current[:half]
    right = jnp.concatenate([current[half:], geometry], 0)
    payload = jnp.concatenate([left, right], 1).astype(BF16)
    for copy in range(payload_ref.shape[0]):
        payload_ref[copy] = payload
    points, rules = weight_ref.shape
    rule = rule_ref[...]
    rows = []
    for point in range(points):
        offsets = [jnp.zeros(rule.shape, F32) for _ in range(3)]
        weight = jnp.zeros(rule.shape, F32)
        for number in range(rules):
            here = rule == number
            for axis in range(3):
                offsets[axis] = jnp.where(here, offset_ref[axis, point, number], offsets[axis])
            weight = jnp.where(here, weight_ref[point, number], weight)
        rows += [blank_ref[pl.ds(axis, 1), :] + offsets[axis] for axis in range(3)]
        rows.append(weight)
    rows.append(cond_ref[...])
    rows.append(jnp.zeros((tile_ref.shape[0] - len(rows), rule.shape[1]), F32))
    tile_ref[...] = jnp.concatenate(rows, 0)


def blank_features(points, *refs):
    tiles, (feature_ref, row_ref) = refs[:-2], refs[-2:]
    whole = jnp.concatenate([tile[...] for tile in tiles], 1)
    width = whole.shape[1]
    for point in range(points):
        place = [whole[4 * point + axis : 4 * point + axis + 1] for axis in range(3)]
        square = place[0] * place[0] + place[1] * place[1] + place[2] * place[2]
        parts = [parts_of(value) for value in place]
        rows = []
        for level in range(3):
            for axis in range(3):
                rows += [-2.0 * parts[axis][level]] * 3
            rows += [jnp.full((1, width), 1.0 if level == 0 else 0.0, F32)] * 3
            rows.append(jnp.zeros((SLOT - 12, width), F32))
        rows += parts_of(square)
        rows.append(jnp.zeros((SLOT - 3, width), F32))
        feature_ref[point] = jnp.concatenate(rows, 0).astype(BF16)
    row_ref[...] = whole


def group_rows(payload, group):
    at = SUBLANES * (group % 3)
    rows = payload[:, at : at + SUBLANES, :]
    return rows.reshape(rows.shape[0] * SUBLANES, LANES)


def coil_features(geometry, group):
    lane = lax.broadcasted_iota(jnp.int32, geometry.shape, 1)
    at = LANES // 2 + 12 * group
    copies = [pltpu.roll(geometry, (SLOT * slot - at) % LANES, 1) for slot in range(3)]
    out = jnp.where(lane < SLOT, copies[0], jnp.where(lane < 2 * SLOT, copies[1], copies[2]))
    return jnp.where(lane < 3 * SLOT, out, 1.0).astype(BF16)


def form(first, payload_ref, feature_ref, row_ref, *refs):
    if first:
        kernel_ref, out_ref = refs
    else:
        before_ref, kernel_ref, out_ref = refs
    samples = out_ref.shape[0]
    points = feature_ref.shape[0]
    groups = kernel_ref.shape[0]
    payload = payload_ref[...]
    geometry = group_rows(payload, 2).astype(F32)
    total = None if first else before_ref[...]
    for group in range(groups):
        coils = coil_features(geometry, group)
        block = None
        for point in range(points):
            squared = jnp.dot(coils, feature_ref[point], preferred_element_type=F32)
            term = row_ref[pl.ds(4 * point + 3, 1), :] * lax.rsqrt(squared)
            block = term if block is None else block + term
        block = block.astype(BF16)
        kernel_ref[group] = block
        product = lax.dot_general(
            group_rows(payload, group), block, (((0,), (0,)), ((), ())), preferred_element_type=F32
        )
        product = product[:samples] if group < 3 else product[samples:]
        total = product if total is None else total + product
    out_ref[...] = total.astype(out_ref.dtype)


def contract(kernel_ref, weighted):
    groups = kernel_ref.shape[0]
    twice = jnp.concatenate([weighted, weighted], 0)
    whole = [
        lax.dot_general(
            kernel_ref[group], twice, (((1,), (1,)), ((), ())), preferred_element_type=F32
        )
        for group in range(groups)
    ]
    lane = lax.broadcasted_iota(jnp.int32, whole[0].shape, 1)
    rows = []
    for group in range(3):
        other = whole[group + 3] if group + 3 < groups else jnp.zeros_like(whole[group])
        both = jnp.where(lane < LANES // 2, whole[group], other)
        rows.append(both.reshape(both.shape[0] // SUBLANES, SUBLANES, LANES))
    return jnp.concatenate(rows, 1)


def weigh(scale, row_ref, *refs):
    arrivals = refs[:-4]
    kernel_ref, current_ref, weighted_ref, out_ref = refs[-4:]
    count = len(arrivals)
    width = current_ref.shape[1]
    blocks = []
    for block in range(count):
        total = None
        for flip in range(count):
            piece = arrivals[flip][:, pl.ds((block ^ flip) * width, width)].astype(F32)
            total = piece if total is None else total + piece
        blocks.append(total.astype(BF16))
    current_ref[...] = blocks[0]
    current = jnp.concatenate(blocks, 1).astype(F32)
    weighted = (row_ref[pl.ds(8, 1), :] * current).astype(BF16)
    weighted_ref[...] = weighted
    out_ref[...] = (scale * contract(kernel_ref, weighted)).astype(out_ref.dtype)


def react(scale, weighted_ref, kernel_ref, out_ref):
    out_ref[...] = scale * contract(kernel_ref, weighted_ref[...])


def finish(arrived_ref, out_ref):
    total = jnp.sum(arrived_ref[...].astype(F32), 0)
    half, samples = total.shape[0], out_ref.shape[1]
    out_ref[...] = jnp.concatenate(
        [total[:, :samples], total[: out_ref.shape[0] - half, samples:]], 0
    )


def from_partner(value, axis, flip):
    size = lax.axis_size(axis)
    return lax.ppermute(value, axis, [(i, i ^ flip) for i in range(size)])


def shaped(shape, dtype):
    return jax.ShapeDtypeStruct(shape, dtype)


def per_device(
    coil_pos, coil_radius, coil_current, blank_pos, blank_rule, blank_cond, quad_offset, quad_weight
):
    samples, coils = coil_current.shape
    blanks = blank_pos.shape[1]
    total_blanks = blanks * lax.axis_size(AXES)
    cols = lax.axis_size(COLS)
    rows = lax.axis_size(ROWS)
    points = quad_weight.shape[1]
    width = rows * blanks
    packed = (cols, 24, LANES)
    kernel_shape = shaped((coils // SUBLANES, cols * SUBLANES, width), BF16)
    smem = pl.BlockSpec(memory_space=pltpu.SMEM)
    vmem = pl.BlockSpec(memory_space=pltpu.VMEM)

    payload, tile = pl.pallas_call(
        prepare,
        out_shape=(shaped(packed, BF16), shaped((16, blanks), F32)),
        in_specs=[smem, smem] + [vmem] * 6,
        name="prepare",
    )(
        quad_offset.transpose(0, 2, 1),
        quad_weight.T,
        coil_pos,
        coil_radius[None, :],
        coil_current.T,
        blank_pos,
        blank_rule[None, :],
        blank_cond[None, :],
    )
    own = lax.all_to_all(payload, COLS, 0, 0, tiled=True)
    tiles = [tile] + [from_partner(tile, ROWS, flip) for flip in range(1, rows)]
    features, table = pl.pallas_call(
        lambda *refs: blank_features(points, *refs),
        out_shape=(shaped((points, LANES, width), BF16), shaped((16, width), F32)),
        compiler_params=ROOM,
        name="blank_features",
    )(*tiles)
    own, features, table = lax.optimization_barrier((own, features, table))
    other = from_partner(own, "core", 1)
    held = cols * coils
    cost = pl.CostEstimate(
        flops=2 * held * width * LANES * (points + 1),
        transcendentals=points * held * width,
        bytes_accessed=2 * held * (width + LANES),
    )
    own_kernel, partial = pl.pallas_call(
        lambda *refs: form(True, *refs),
        out_shape=(kernel_shape, shaped((samples, width), F32)),
        compiler_params=ROOM,
        cost_estimate=cost,
        name="form_own",
    )(own, features, table)
    other_kernel, partial = pl.pallas_call(
        lambda *refs: form(False, *refs),
        out_shape=(kernel_shape, shaped((samples, width), BF16)),
        compiler_params=ROOM,
        cost_estimate=cost,
        name="form_other",
    )(other, features, table, partial)

    arrivals = [partial] + [from_partner(partial, ROWS, flip) for flip in range(1, rows)]
    scale = 2.0 / total_blanks
    react_cost = pl.CostEstimate(
        flops=2 * held * width * samples,
        transcendentals=0,
        bytes_accessed=2 * held * (width + 2 * samples),
    )
    blank_current, weighted, reaction = pl.pallas_call(
        lambda *refs: weigh(scale, *refs),
        out_shape=(
            shaped((samples, blanks), BF16),
            shaped((samples, width), BF16),
            shaped(packed, BF16),
        ),
        compiler_params=ROOM,
        cost_estimate=react_cost,
        name="weigh",
    )(table, *arrivals, other_kernel)
    crossed = from_partner(reaction, "core", 1)
    reaction = pl.pallas_call(
        lambda *refs: react(scale, *refs),
        out_shape=shaped(packed, F32),
        compiler_params=ROOM,
        cost_estimate=react_cost,
        name="react",
    )(weighted, own_kernel)
    pieces = (reaction + crossed.astype(F32)).astype(BF16)
    arrived = lax.all_to_all(pieces, COLS, 0, 0, tiled=True)
    coil_reaction = pl.pallas_call(
        finish,
        out_shape=shaped((coils, samples), F32),
        compiler_params=ROOM,
        name="finish",
    )(arrived)
    return (blank_current, coil_reaction.T)


def solution(mesh):
    split = Mesh(mesh.devices.reshape(SIZES), AXES)
    whole = P(None, AXES)
    return jax.shard_map(
        per_device,
        mesh=split,
        in_specs=(whole, P(AXES), whole, whole, P(AXES), P(AXES), P(), P()),
        out_specs=(whole, whole),
        check_vma=False,
    )
```

```python
import jax
import jax.numpy as jnp
from jax import lax
from jax.experimental import pallas as pl
from jax.experimental.pallas import tpu as pltpu
from jax.sharding import Mesh
from jax.sharding import PartitionSpec as P

AXES = ("zh", "zl", "xh", "y", "xl", "core")
SIZES = (4, 2, 2, 4, 2, 2)
ROWS = ("y",)
COLS = ("xh", "xl", "zh", "zl")
LANES = 128
SUBLANES = 8
SLOT = 32
BF16 = jnp.bfloat16
F32 = jnp.float32
ROOM = pltpu.CompilerParams(vmem_limit_bytes=16 << 20)


def parts_of(value):
    high = value.astype(BF16).astype(F32)
    rest = value - high
    mid = rest.astype(BF16).astype(F32)
    low = (rest - mid).astype(BF16).astype(F32)
    return [high, mid, low]


def prepare(
    offset_ref,
    weight_ref,
    pos_ref,
    radius_ref,
    current_ref,
    blank_ref,
    rule_ref,
    cond_ref,
    payload_ref,
    tile_ref,
):
    coils, samples = current_ref.shape
    groups = coils // SUBLANES
    x, y, z = (pos_ref[pl.ds(axis, 1), :] for axis in range(3))
    radius = radius_ref[...]
    square = x * x + y * y + z * z + radius * radius
    rows = [part for value in (x, y, z, square) for part in parts_of(value)]
    count = len(rows)
    rows.append(jnp.zeros((16 - count, coils), F32))
    columns = jnp.concatenate(rows, 0).T
    geometry = [columns[SUBLANES * g : SUBLANES * (g + 1), :count] for g in range(groups)]
    geometry.append(jnp.zeros((SUBLANES, samples - count * groups), F32))
    geometry = jnp.concatenate(geometry, 1)
    current = current_ref[...].astype(F32)
    half = payload_ref.shape[1]
    left = current[:half]
    right = jnp.concatenate([current[half:], geometry], 0)
    payload = jnp.concatenate([left, right], 1).astype(BF16)
    for copy in range(payload_ref.shape[0]):
        payload_ref[copy] = payload
    points, rules = weight_ref.shape
    rule = rule_ref[...]
    rows = []
    for point in range(points):
        offsets = [jnp.zeros(rule.shape, F32) for _ in range(3)]
        weight = jnp.zeros(rule.shape, F32)
        for number in range(rules):
            here = rule == number
            for axis in range(3):
                offsets[axis] = jnp.where(here, offset_ref[axis, point, number], offsets[axis])
            weight = jnp.where(here, weight_ref[point, number], weight)
        rows += [blank_ref[pl.ds(axis, 1), :] + offsets[axis] for axis in range(3)]
        rows.append(weight)
    rows.append(cond_ref[...])
    rows.append(jnp.zeros((tile_ref.shape[0] - len(rows), rule.shape[1]), F32))
    tile_ref[...] = jnp.concatenate(rows, 0)


def blank_features(points, *refs):
    tiles, (feature_ref, row_ref) = refs[:-2], refs[-2:]
    whole = jnp.concatenate([tile[...] for tile in tiles], 1)
    width = whole.shape[1]
    for point in range(points):
        place = [whole[4 * point + axis : 4 * point + axis + 1] for axis in range(3)]
        square = place[0] * place[0] + place[1] * place[1] + place[2] * place[2]
        parts = [parts_of(value) for value in place]
        rows = []
        for level in range(3):
            for axis in range(3):
                rows += [-2.0 * parts[axis][level]] * 3
            rows += [jnp.full((1, width), 1.0 if level == 0 else 0.0, F32)] * 3
            rows.append(jnp.zeros((SLOT - 12, width), F32))
        rows += parts_of(square)
        rows.append(jnp.zeros((SLOT - 3, width), F32))
        feature_ref[point] = jnp.concatenate(rows, 0).astype(BF16)
    row_ref[...] = whole


def group_rows(payload, group):
    at = SUBLANES * (group % 3)
    rows = payload[:, at : at + SUBLANES, :]
    return rows.reshape(rows.shape[0] * SUBLANES, LANES)


def coil_features(geometry, group):
    lane = lax.broadcasted_iota(jnp.int32, geometry.shape, 1)
    at = LANES // 2 + 12 * group
    copies = [pltpu.roll(geometry, (SLOT * slot - at) % LANES, 1) for slot in range(3)]
    out = jnp.where(lane < SLOT, copies[0], jnp.where(lane < 2 * SLOT, copies[1], copies[2]))
    return jnp.where(lane < 3 * SLOT, out, 1.0).astype(BF16)


def form(first, payload_ref, feature_ref, row_ref, *refs):
    if first:
        kernel_ref, out_ref = refs
    else:
        before_ref, kernel_ref, out_ref = refs
    samples = out_ref.shape[0]
    points = feature_ref.shape[0]
    groups = kernel_ref.shape[0]
    payload = payload_ref[...]
    geometry = group_rows(payload, 2).astype(F32)
    for group in range(groups):
        coils = coil_features(geometry, group)
        block = None
        for point in range(points):
            squared = jnp.dot(coils, feature_ref[point], preferred_element_type=F32)
            term = row_ref[pl.ds(4 * point + 3, 1), :] * lax.rsqrt(squared)
            block = term if block is None else block + term
        kernel_ref[group] = block.astype(BF16)
    turned = [group_rows(payload, group).T for group in range(3)]
    current = [
        turned[group % 3][:samples] if group < 3 else turned[group % 3][samples:]
        for group in range(groups)
    ]
    kernel = kernel_ref[...].reshape(groups * kernel_ref.shape[1], kernel_ref.shape[2])
    total = jnp.dot(jnp.concatenate(current, 1), kernel, preferred_element_type=F32)
    if not first:
        total = total + before_ref[...]
    out_ref[...] = total.astype(out_ref.dtype)


def contract(kernel_ref, weighted):
    groups = kernel_ref.shape[0]
    twice = jnp.concatenate([weighted, weighted], 0)
    whole = [
        lax.dot_general(
            kernel_ref[group], twice, (((1,), (1,)), ((), ())), preferred_element_type=F32
        )
        for group in range(groups)
    ]
    shards = whole[0].shape[0] // SUBLANES
    whole = [part.reshape(shards, SUBLANES, LANES) for part in whole]
    lane = lax.broadcasted_iota(jnp.int32, whole[0].shape, 2)
    others = [whole[3], whole[4], pltpu.roll(whole[2], SUBLANES // 2, 1)]
    return [jnp.where(lane < LANES // 2, whole[group], others[group]) for group in range(3)]


def store_rows(out_ref, groups):
    for pair in range(out_ref.shape[2] // LANES):
        at = 2 * (pair % 4)
        rows = groups[pair // 4][:, at : at + 2, :]
        out_ref[:, :, pl.ds(pair * LANES, LANES)] = rows.astype(out_ref.dtype)


def weigh(scale, row_ref, *refs):
    arrivals = refs[:-4]
    kernel_ref, current_ref, weighted_ref, out_ref = refs[-4:]
    count = len(arrivals)
    width = current_ref.shape[1]
    blocks = []
    for block in range(count):
        total = None
        for flip in range(count):
            piece = arrivals[flip][:, pl.ds((block ^ flip) * width, width)].astype(F32)
            total = piece if total is None else total + piece
        blocks.append(total.astype(BF16))
    current_ref[...] = blocks[0]
    current = jnp.concatenate(blocks, 1).astype(F32)
    weighted = (row_ref[pl.ds(8, 1), :] * current).astype(BF16)
    weighted_ref[...] = weighted
    store_rows(out_ref, [scale * part for part in contract(kernel_ref, weighted)])


def react(scale, weighted_ref, kernel_ref, current_ref, out_ref, blank_ref):
    store_rows(out_ref, [scale * part for part in contract(kernel_ref, weighted_ref[...])])
    blank_ref[...] = current_ref[...]


def finish(arrived_ref, out_ref):
    total = jnp.sum(arrived_ref[...].astype(F32), 0)
    rows = [total[:, LANES * pair : LANES * (pair + 1)] for pair in range(total.shape[1] // LANES)]
    rows = jnp.concatenate(rows, 0)
    samples = out_ref.shape[1]
    out_ref[...] = jnp.concatenate(
        [rows[:, :samples], rows[16:, samples:], rows[:16, samples:]], 0
    )


def from_partner(value, axis, flip):
    size = lax.axis_size(axis)
    return lax.ppermute(value, axis, [(i, i ^ flip) for i in range(size)])


def shaped(shape, dtype):
    return jax.ShapeDtypeStruct(shape, dtype)


def per_device(
    coil_pos, coil_radius, coil_current, blank_pos, blank_rule, blank_cond, quad_offset, quad_weight
):
    samples, coils = coil_current.shape
    blanks = blank_pos.shape[1]
    total_blanks = blanks * lax.axis_size(AXES)
    cols = lax.axis_size(COLS)
    rows = lax.axis_size(ROWS)
    points = quad_weight.shape[1]
    width = rows * blanks
    packed = (cols, 24, LANES)
    dense = (cols, 2, coils * samples // 2)
    kernel_shape = shaped((coils // SUBLANES, cols * SUBLANES, width), BF16)
    smem = pl.BlockSpec(memory_space=pltpu.SMEM)
    vmem = pl.BlockSpec(memory_space=pltpu.VMEM)

    payload, tile = pl.pallas_call(
        prepare,
        out_shape=(shaped(packed, BF16), shaped((16, blanks), F32)),
        in_specs=[smem, smem] + [vmem] * 6,
        name="prepare",
    )(
        quad_offset.transpose(0, 2, 1),
        quad_weight.T,
        coil_pos,
        coil_radius[None, :],
        coil_current.T,
        blank_pos,
        blank_rule[None, :],
        blank_cond[None, :],
    )
    own = lax.all_to_all(payload, COLS, 0, 0, tiled=True)
    tiles = [tile] + [from_partner(tile, ROWS, flip) for flip in range(1, rows)]
    features, table = pl.pallas_call(
        lambda *refs: blank_features(points, *refs),
        out_shape=(shaped((points, LANES, width), BF16), shaped((16, width), F32)),
        compiler_params=ROOM,
        name="blank_features",
    )(*tiles)
    own, features, table = lax.optimization_barrier((own, features, table))
    other = from_partner(own, "core", 1)
    held = cols * coils
    cost = pl.CostEstimate(
        flops=2 * held * width * LANES * (points + 1),
        transcendentals=points * held * width,
        bytes_accessed=2 * held * (width + LANES),
    )
    own_kernel, partial = pl.pallas_call(
        lambda *refs: form(True, *refs),
        out_shape=(kernel_shape, shaped((samples, width), F32)),
        compiler_params=ROOM,
        cost_estimate=cost,
        name="form_own",
    )(own, features, table)
    other_kernel, partial = pl.pallas_call(
        lambda *refs: form(False, *refs),
        out_shape=(kernel_shape, shaped((samples, width), BF16)),
        compiler_params=ROOM,
        cost_estimate=cost,
        name="form_other",
    )(other, features, table, partial)

    arrivals = [partial] + [from_partner(partial, ROWS, flip) for flip in range(1, rows)]
    scale = 2.0 / total_blanks
    react_cost = pl.CostEstimate(
        flops=2 * held * width * samples,
        transcendentals=0,
        bytes_accessed=2 * held * (width + 2 * samples),
    )
    blank_current, weighted, reaction = pl.pallas_call(
        lambda *refs: weigh(scale, *refs),
        out_shape=(
            shaped((samples, blanks), BF16),
            shaped((samples, width), BF16),
            shaped(dense, BF16),
        ),
        compiler_params=ROOM,
        cost_estimate=react_cost,
        name="weigh",
    )(table, *arrivals, other_kernel)
    crossed = from_partner(reaction, "core", 1)
    reaction, blank_current = pl.pallas_call(
        lambda *refs: react(scale, *refs),
        out_shape=(shaped(dense, F32), shaped((samples, blanks), BF16)),
        compiler_params=ROOM,
        cost_estimate=react_cost,
        name="react",
    )(weighted, own_kernel, blank_current)
    pieces = (reaction + crossed.astype(F32)).astype(BF16)
    arrived = lax.all_to_all(pieces, COLS, 0, 0, tiled=True)
    coil_reaction = pl.pallas_call(
        finish,
        out_shape=shaped((coils, samples), F32),
        compiler_params=ROOM,
        name="finish",
    )(arrived)
    return (blank_current, coil_reaction.T)


def solution(mesh):
    split = Mesh(mesh.devices.reshape(SIZES), AXES)
    whole = P(None, AXES)
    return jax.shard_map(
        per_device,
        mesh=split,
        in_specs=(whole, P(AXES), whole, whole, P(AXES), P(AXES), P(), P()),
        out_specs=(whole, whole),
        check_vma=False,
    )
```

```python
import jax
import jax.numpy as jnp
from jax import lax
from jax.experimental import pallas as pl
from jax.experimental.pallas import tpu as pltpu
from jax.sharding import Mesh
from jax.sharding import PartitionSpec as P

AXES = ("zh", "zl", "xh", "y", "xl", "core")
SIZES = (4, 2, 2, 4, 2, 2)
ROWS = ("y",)
COLS = ("xh", "xl", "zh", "zl")
LANES = 128
SUBLANES = 8
SLOT = 32
BF16 = jnp.bfloat16
F32 = jnp.float32
ROOM = pltpu.CompilerParams(vmem_limit_bytes=16 << 20)


def parts_of(value):
    high = value.astype(BF16).astype(F32)
    rest = value - high
    mid = rest.astype(BF16).astype(F32)
    low = (rest - mid).astype(BF16).astype(F32)
    return [high, mid, low]


def prepare(
    offset_ref,
    weight_ref,
    pos_ref,
    radius_ref,
    current_ref,
    blank_ref,
    rule_ref,
    cond_ref,
    payload_ref,
    tile_ref,
):
    coils, samples = current_ref.shape
    groups = coils // SUBLANES
    x, y, z = (pos_ref[pl.ds(axis, 1), :] for axis in range(3))
    radius = radius_ref[...]
    square = x * x + y * y + z * z + radius * radius
    rows = [part for value in (x, y, z, square) for part in parts_of(value)]
    count = len(rows)
    rows.append(jnp.zeros((16 - count, coils), F32))
    columns = jnp.concatenate(rows, 0).T
    geometry = [columns[SUBLANES * g : SUBLANES * (g + 1), :count] for g in range(groups)]
    geometry.append(jnp.zeros((SUBLANES, samples - count * groups), F32))
    geometry = jnp.concatenate(geometry, 1)
    current = current_ref[...].astype(F32)
    half = payload_ref.shape[1]
    left = current[:half]
    right = jnp.concatenate([current[half:], geometry], 0)
    payload = jnp.concatenate([left, right], 1).astype(BF16)
    for copy in range(payload_ref.shape[0]):
        payload_ref[copy] = payload
    points, rules = weight_ref.shape
    rule = rule_ref[...]
    rows = []
    for point in range(points):
        offsets = [jnp.zeros(rule.shape, F32) for _ in range(3)]
        weight = jnp.zeros(rule.shape, F32)
        for number in range(rules):
            here = rule == number
            for axis in range(3):
                offsets[axis] = jnp.where(here, offset_ref[axis, point, number], offsets[axis])
            weight = jnp.where(here, weight_ref[point, number], weight)
        rows += [blank_ref[pl.ds(axis, 1), :] + offsets[axis] for axis in range(3)]
        rows.append(weight)
    rows.append(cond_ref[...])
    rows.append(jnp.zeros((tile_ref.shape[0] - len(rows), rule.shape[1]), F32))
    tile_ref[...] = jnp.concatenate(rows, 0)


def blank_features(points, *refs):
    tiles, (feature_ref, row_ref) = refs[:-2], refs[-2:]
    whole = jnp.concatenate([tile[...] for tile in tiles], 1)
    width = whole.shape[1]
    for point in range(points):
        place = [whole[4 * point + axis : 4 * point + axis + 1] for axis in range(3)]
        square = place[0] * place[0] + place[1] * place[1] + place[2] * place[2]
        parts = [parts_of(value) for value in place]
        rows = []
        for level in range(3):
            for axis in range(3):
                rows += [-2.0 * parts[axis][level]] * 3
            rows += [jnp.full((1, width), 1.0 if level == 0 else 0.0, F32)] * 3
            rows.append(jnp.zeros((SLOT - 12, width), F32))
        rows += parts_of(square)
        rows.append(jnp.zeros((SLOT - 3, width), F32))
        feature_ref[point] = jnp.concatenate(rows, 0).astype(BF16)
    row_ref[...] = whole


def group_rows(payload, group):
    at = SUBLANES * (group % 3)
    rows = payload[:, at : at + SUBLANES, :]
    return rows.reshape(rows.shape[0] * SUBLANES, LANES)


def coil_features(geometry, group):
    lane = lax.broadcasted_iota(jnp.int32, geometry.shape, 1)
    at = LANES // 2 + 12 * group
    copies = [pltpu.roll(geometry, (SLOT * slot - at) % LANES, 1) for slot in range(3)]
    out = jnp.where(lane < SLOT, copies[0], jnp.where(lane < 2 * SLOT, copies[1], copies[2]))
    return jnp.where(lane < 3 * SLOT, out, 1.0).astype(BF16)


def form(first, payload_ref, feature_ref, row_ref, *refs):
    if first:
        kernel_ref, out_ref = refs
    else:
        before_ref, kernel_ref, out_ref = refs
    samples = out_ref.shape[0]
    points = feature_ref.shape[0]
    groups = kernel_ref.shape[0]
    payload = payload_ref[...]
    geometry = group_rows(payload, 2).astype(F32)
    for group in range(groups):
        coils = coil_features(geometry, group)
        block = None
        for point in range(points):
            squared = jnp.dot(coils, feature_ref[point], preferred_element_type=F32)
            term = row_ref[pl.ds(4 * point + 3, 1), :] * lax.rsqrt(squared)
            block = term if block is None else block + term
        kernel_ref[group] = block.astype(BF16)
    turned = [group_rows(payload, group).T for group in range(3)]
    current = [
        turned[group % 3][:samples] if group < 3 else turned[group % 3][samples:]
        for group in range(groups)
    ]
    kernel = kernel_ref[...].reshape(groups * kernel_ref.shape[1], kernel_ref.shape[2])
    total = jnp.dot(jnp.concatenate(current, 1), kernel, preferred_element_type=F32)
    if not first:
        total = total + before_ref[...]
    out_ref[...] = total.astype(out_ref.dtype)


def contract(kernel_ref, weighted):
    groups = kernel_ref.shape[0]
    twice = jnp.concatenate([weighted, weighted], 0)
    whole = [
        lax.dot_general(
            kernel_ref[group], twice, (((1,), (1,)), ((), ())), preferred_element_type=F32
        )
        for group in range(groups)
    ]
    shards = whole[0].shape[0] // SUBLANES
    whole = [part.reshape(shards, SUBLANES, LANES) for part in whole]
    lane = lax.broadcasted_iota(jnp.int32, whole[0].shape, 2)
    others = [whole[3], whole[4], pltpu.roll(whole[2], SUBLANES // 2, 1)]
    return [jnp.where(lane < LANES // 2, whole[group], others[group]) for group in range(3)]


def store_rows(out_ref, groups):
    for pair in range(out_ref.shape[2] // LANES):
        at = 2 * (pair % 4)
        rows = groups[pair // 4][:, at : at + 2, :]
        out_ref[:, :, pl.ds(pair * LANES, LANES)] = rows.astype(out_ref.dtype)


def weigh(scale, row_ref, *refs):
    arrivals = refs[:-4]
    kernel_ref, current_ref, weighted_ref, out_ref = refs[-4:]
    count = len(arrivals)
    width = current_ref.shape[1]
    blocks = []
    for block in range(count):
        total = None
        for flip in range(count):
            piece = arrivals[flip][:, pl.ds((block ^ flip) * width, width)].astype(F32)
            total = piece if total is None else total + piece
        blocks.append(total.astype(BF16))
    current_ref[...] = blocks[0]
    current = jnp.concatenate(blocks, 1).astype(F32)
    weighted = (row_ref[pl.ds(8, 1), :] * current).astype(BF16)
    weighted_ref[...] = weighted
    store_rows(out_ref, [scale * part for part in contract(kernel_ref, weighted)])


def react(scale, weighted_ref, kernel_ref, current_ref, out_ref, blank_ref):
    store_rows(out_ref, [scale * part for part in contract(kernel_ref, weighted_ref[...])])
    blank_ref[...] = current_ref[...]


def finish(arrived_ref, out_ref):
    total = jnp.sum(arrived_ref[...].astype(F32), 0)
    rows = [total[:, LANES * pair : LANES * (pair + 1)] for pair in range(total.shape[1] // LANES)]
    rows = jnp.concatenate(rows, 0)
    samples = out_ref.shape[1]
    out_ref[...] = jnp.concatenate(
        [rows[:, :samples], rows[16:, samples:], rows[:16, samples:]], 0
    )


def from_partner(value, axis, flip):
    size = lax.axis_size(axis)
    return lax.ppermute(value, axis, [(i, i ^ flip) for i in range(size)])


def shaped(shape, dtype):
    return jax.ShapeDtypeStruct(shape, dtype)


def per_device(
    coil_pos, coil_radius, coil_current, blank_pos, blank_rule, blank_cond, quad_offset, quad_weight
):
    samples, coils = coil_current.shape
    blanks = blank_pos.shape[1]
    total_blanks = blanks * lax.axis_size(AXES)
    cols = lax.axis_size(COLS)
    rows = lax.axis_size(ROWS)
    points = quad_weight.shape[1]
    width = rows * blanks
    packed = (cols, 24, LANES)
    dense = (cols, 2, coils * samples // 2)
    kernel_shape = shaped((coils // SUBLANES, cols * SUBLANES, width), BF16)
    smem = pl.BlockSpec(memory_space=pltpu.SMEM)
    vmem = pl.BlockSpec(memory_space=pltpu.VMEM)

    arguments = (
        quad_offset.transpose(0, 2, 1),
        quad_weight.T,
        coil_pos,
        coil_radius[None, :],
        coil_current.T,
        blank_pos,
        blank_rule[None, :],
        blank_cond[None, :],
    )
    payload, tile = pl.pallas_call(
        prepare,
        out_shape=(shaped(packed, BF16), shaped((16, blanks), F32)),
        in_specs=[smem, smem] + [vmem] * 6,
        compiler_params=ROOM,
        name="prepare",
    )(*(pltpu.with_memory_space_constraint(value, pltpu.HBM) for value in arguments))
    own = lax.all_to_all(payload, COLS, 0, 0, tiled=True)
    tiles = [tile] + [from_partner(tile, ROWS, flip) for flip in range(1, rows)]
    features, table = pl.pallas_call(
        lambda *refs: blank_features(points, *refs),
        out_shape=(shaped((points, LANES, width), BF16), shaped((16, width), F32)),
        compiler_params=ROOM,
        name="blank_features",
    )(*tiles)
    own, features, table = lax.optimization_barrier((own, features, table))
    other = from_partner(own, "core", 1)
    held = cols * coils
    cost = pl.CostEstimate(
        flops=2 * held * width * LANES * (points + 1),
        transcendentals=points * held * width,
        bytes_accessed=2 * held * (width + LANES),
    )
    own_kernel, partial = pl.pallas_call(
        lambda *refs: form(True, *refs),
        out_shape=(kernel_shape, shaped((samples, width), F32)),
        compiler_params=ROOM,
        cost_estimate=cost,
        name="form_own",
    )(own, features, table)
    other_kernel, partial = pl.pallas_call(
        lambda *refs: form(False, *refs),
        out_shape=(kernel_shape, shaped((samples, width), BF16)),
        compiler_params=ROOM,
        cost_estimate=cost,
        name="form_other",
    )(other, features, table, partial)

    arrivals = [partial] + [from_partner(partial, ROWS, flip) for flip in range(1, rows)]
    scale = 2.0 / total_blanks
    react_cost = pl.CostEstimate(
        flops=2 * held * width * samples,
        transcendentals=0,
        bytes_accessed=2 * held * (width + 2 * samples),
    )
    blank_current, weighted, reaction = pl.pallas_call(
        lambda *refs: weigh(scale, *refs),
        out_shape=(
            shaped((samples, blanks), BF16),
            shaped((samples, width), BF16),
            shaped(dense, BF16),
        ),
        compiler_params=ROOM,
        cost_estimate=react_cost,
        name="weigh",
    )(table, *arrivals, other_kernel)
    crossed = from_partner(reaction, "core", 1)
    reaction, blank_current = pl.pallas_call(
        lambda *refs: react(scale, *refs),
        out_shape=(shaped(dense, F32), shaped((samples, blanks), BF16)),
        compiler_params=ROOM,
        cost_estimate=react_cost,
        name="react",
    )(weighted, own_kernel, blank_current)
    pieces = (reaction + crossed.astype(F32)).astype(BF16)
    arrived = lax.all_to_all(pieces, COLS, 0, 0, tiled=True)
    coil_reaction = pl.pallas_call(
        finish,
        out_shape=shaped((coils, samples), F32),
        compiler_params=ROOM,
        name="finish",
    )(arrived)
    return (blank_current, coil_reaction.T)


def solution(mesh):
    split = Mesh(mesh.devices.reshape(SIZES), AXES)
    whole = P(None, AXES)
    return jax.shard_map(
        per_device,
        mesh=split,
        in_specs=(whole, P(AXES), whole, whole, P(AXES), P(AXES), P(), P()),
        out_specs=(whole, whole),
        check_vma=False,
    )
```

```python
import jax
import jax.numpy as jnp
from jax import lax
from jax.experimental import pallas as pl
from jax.experimental.pallas import tpu as pltpu
from jax.sharding import Mesh
from jax.sharding import PartitionSpec as P

AXES = ("zh", "zl", "xh", "y", "xl", "core")
SIZES = (4, 2, 2, 4, 2, 2)
ROWS = ("xh", "xl")
COLS = ("zl", "y", "zh")
LANES = 128
SUBLANES = 8
SLOT = 32
BF16 = jnp.bfloat16
F32 = jnp.float32
ROOM = pltpu.CompilerParams(vmem_limit_bytes=16 << 20)


def parts_of(value):
    high = value.astype(BF16).astype(F32)
    rest = value - high
    mid = rest.astype(BF16).astype(F32)
    low = (rest - mid).astype(BF16).astype(F32)
    return [high, mid, low]


def prepare(
    offset_ref,
    weight_ref,
    pos_ref,
    radius_ref,
    current_ref,
    blank_ref,
    rule_ref,
    cond_ref,
    payload_ref,
    tile_ref,
):
    coils, samples = current_ref.shape
    groups = coils // SUBLANES
    x, y, z = (pos_ref[pl.ds(axis, 1), :] for axis in range(3))
    radius = radius_ref[...]
    square = x * x + y * y + z * z + radius * radius
    rows = [part for value in (x, y, z, square) for part in parts_of(value)]
    count = len(rows)
    rows.append(jnp.zeros((16 - count, coils), F32))
    columns = jnp.concatenate(rows, 0).T
    geometry = [columns[SUBLANES * g : SUBLANES * (g + 1), :count] for g in range(groups)]
    geometry.append(jnp.zeros((SUBLANES, samples - count * groups), F32))
    geometry = jnp.concatenate(geometry, 1)
    current = current_ref[...].astype(F32)
    half = payload_ref.shape[1]
    left = current[:half]
    right = jnp.concatenate([current[half:], geometry], 0)
    payload = jnp.concatenate([left, right], 1).astype(BF16)
    for copy in range(payload_ref.shape[0]):
        payload_ref[copy] = payload
    points, rules = weight_ref.shape
    rule = rule_ref[...]
    rows = []
    for point in range(points):
        offsets = [jnp.zeros(rule.shape, F32) for _ in range(3)]
        weight = jnp.zeros(rule.shape, F32)
        for number in range(rules):
            here = rule == number
            for axis in range(3):
                offsets[axis] = jnp.where(here, offset_ref[axis, point, number], offsets[axis])
            weight = jnp.where(here, weight_ref[point, number], weight)
        rows += [blank_ref[pl.ds(axis, 1), :] + offsets[axis] for axis in range(3)]
        rows.append(weight)
    rows.append(cond_ref[...])
    rows.append(jnp.zeros((tile_ref.shape[0] - len(rows), rule.shape[1]), F32))
    tile_ref[...] = jnp.concatenate(rows, 0)


def blank_features(points, *refs):
    tiles, (feature_ref, row_ref) = refs[:-2], refs[-2:]
    whole = jnp.concatenate([tile[...] for tile in tiles], 1)
    width = whole.shape[1]
    for point in range(points):
        place = [whole[4 * point + axis : 4 * point + axis + 1] for axis in range(3)]
        square = place[0] * place[0] + place[1] * place[1] + place[2] * place[2]
        parts = [parts_of(value) for value in place]
        rows = []
        for level in range(3):
            for axis in range(3):
                rows += [-2.0 * parts[axis][level]] * 3
            rows += [jnp.full((1, width), 1.0 if level == 0 else 0.0, F32)] * 3
            rows.append(jnp.zeros((SLOT - 12, width), F32))
        rows += parts_of(square)
        rows.append(jnp.zeros((SLOT - 3, width), F32))
        feature_ref[point] = jnp.concatenate(rows, 0).astype(BF16)
    row_ref[...] = whole


def group_rows(payload, group):
    at = SUBLANES * (group % 3)
    rows = payload[:, at : at + SUBLANES, :]
    return rows.reshape(rows.shape[0] * SUBLANES, LANES)


def coil_features(geometry, group):
    lane = lax.broadcasted_iota(jnp.int32, geometry.shape, 1)
    at = LANES // 2 + 12 * group
    copies = [pltpu.roll(geometry, (SLOT * slot - at) % LANES, 1) for slot in range(3)]
    out = jnp.where(lane < SLOT, copies[0], jnp.where(lane < 2 * SLOT, copies[1], copies[2]))
    return jnp.where(lane < 3 * SLOT, out, 1.0).astype(BF16)


def form(first, payload_ref, feature_ref, row_ref, *refs):
    if first:
        kernel_ref, out_ref = refs
    else:
        before_ref, kernel_ref, out_ref = refs
    samples = out_ref.shape[0]
    points = feature_ref.shape[0]
    groups = kernel_ref.shape[0]
    payload = payload_ref[...]
    geometry = group_rows(payload, 2).astype(F32)
    for group in range(groups):
        coils = coil_features(geometry, group)
        block = None
        for point in range(points):
            squared = jnp.dot(coils, feature_ref[point], preferred_element_type=F32)
            term = row_ref[pl.ds(4 * point + 3, 1), :] * lax.rsqrt(squared)
            block = term if block is None else block + term
        kernel_ref[group] = block.astype(BF16)
    turned = [group_rows(payload, group).T for group in range(3)]
    current = [
        turned[group % 3][:samples] if group < 3 else turned[group % 3][samples:]
        for group in range(groups)
    ]
    kernel = kernel_ref[...].reshape(groups * kernel_ref.shape[1], kernel_ref.shape[2])
    total = jnp.dot(jnp.concatenate(current, 1), kernel, preferred_element_type=F32)
    if not first:
        total = total + before_ref[...]
    out_ref[...] = total.astype(out_ref.dtype)


def contract(kernel_ref, weighted):
    groups = kernel_ref.shape[0]
    twice = jnp.concatenate([weighted, weighted], 0)
    whole = [
        lax.dot_general(
            kernel_ref[group], twice, (((1,), (1,)), ((), ())), preferred_element_type=F32
        )
        for group in range(groups)
    ]
    shards = whole[0].shape[0] // SUBLANES
    whole = [part.reshape(shards, SUBLANES, LANES) for part in whole]
    lane = lax.broadcasted_iota(jnp.int32, whole[0].shape, 2)
    others = [whole[3], whole[4], pltpu.roll(whole[2], SUBLANES // 2, 1)]
    return [jnp.where(lane < LANES // 2, whole[group], others[group]) for group in range(3)]


def store_rows(out_ref, groups):
    for pair in range(out_ref.shape[2] // LANES):
        at = 2 * (pair % 4)
        rows = groups[pair // 4][:, at : at + 2, :]
        out_ref[:, :, pl.ds(pair * LANES, LANES)] = rows.astype(out_ref.dtype)


def weigh(scale, row_ref, *refs):
    arrivals = refs[:-4]
    kernel_ref, current_ref, weighted_ref, out_ref = refs[-4:]
    count = len(arrivals)
    width = current_ref.shape[1]
    blocks = []
    for block in range(count):
        total = None
        for flip in range(count):
            piece = arrivals[flip][:, pl.ds((block ^ flip) * width, width)].astype(F32)
            total = piece if total is None else total + piece
        blocks.append(total.astype(BF16))
    current_ref[...] = blocks[0]
    current = jnp.concatenate(blocks, 1).astype(F32)
    weighted = (row_ref[pl.ds(8, 1), :] * current).astype(BF16)
    weighted_ref[...] = weighted
    store_rows(out_ref, [scale * part for part in contract(kernel_ref, weighted)])


def react(scale, weighted_ref, kernel_ref, current_ref, out_ref, blank_ref):
    store_rows(out_ref, [scale * part for part in contract(kernel_ref, weighted_ref[...])])
    blank_ref[...] = current_ref[...]


def finish(arrived_ref, out_ref):
    total = jnp.sum(arrived_ref[...].astype(F32), 0)
    rows = [total[:, LANES * pair : LANES * (pair + 1)] for pair in range(total.shape[1] // LANES)]
    rows = jnp.concatenate(rows, 0)
    samples = out_ref.shape[1]
    out_ref[...] = jnp.concatenate(
        [rows[:, :samples], rows[16:, samples:], rows[:16, samples:]], 0
    )


def from_partner(value, axis, flip):
    size = lax.axis_size(axis)
    return lax.ppermute(value, axis, [(i, i ^ flip) for i in range(size)])


def shaped(shape, dtype):
    return jax.ShapeDtypeStruct(shape, dtype)


def per_device(
    coil_pos, coil_radius, coil_current, blank_pos, blank_rule, blank_cond, quad_offset, quad_weight
):
    samples, coils = coil_current.shape
    blanks = blank_pos.shape[1]
    total_blanks = blanks * lax.axis_size(AXES)
    cols = lax.axis_size(COLS)
    rows = lax.axis_size(ROWS)
    points = quad_weight.shape[1]
    width = rows * blanks
    packed = (cols, 24, LANES)
    dense = (cols, 2, coils * samples // 2)
    kernel_shape = shaped((coils // SUBLANES, cols * SUBLANES, width), BF16)
    smem = pl.BlockSpec(memory_space=pltpu.SMEM)
    vmem = pl.BlockSpec(memory_space=pltpu.VMEM)

    arguments = (
        quad_offset.transpose(0, 2, 1),
        quad_weight.T,
        coil_pos,
        coil_radius[None, :],
        coil_current.T,
        blank_pos,
        blank_rule[None, :],
        blank_cond[None, :],
    )
    payload, tile = pl.pallas_call(
        prepare,
        out_shape=(shaped(packed, BF16), shaped((16, blanks), F32)),
        in_specs=[smem, smem] + [vmem] * 6,
        compiler_params=ROOM,
        name="prepare",
    )(*(pltpu.with_memory_space_constraint(value, pltpu.HBM) for value in arguments))
    own = lax.all_to_all(payload, COLS, 0, 0, tiled=True)
    tiles = [tile] + [from_partner(tile, ROWS, flip) for flip in range(1, rows)]
    features, table = pl.pallas_call(
        lambda *refs: blank_features(points, *refs),
        out_shape=(shaped((points, LANES, width), BF16), shaped((16, width), F32)),
        compiler_params=ROOM,
        name="blank_features",
    )(*tiles)
    own, features, table = lax.optimization_barrier((own, features, table))
    other = from_partner(own, "core", 1)
    held = cols * coils
    cost = pl.CostEstimate(
        flops=2 * held * width * LANES * (points + 1),
        transcendentals=points * held * width,
        bytes_accessed=2 * held * (width + LANES),
    )
    own_kernel, partial = pl.pallas_call(
        lambda *refs: form(True, *refs),
        out_shape=(kernel_shape, shaped((samples, width), F32)),
        compiler_params=ROOM,
        cost_estimate=cost,
        name="form_own",
    )(own, features, table)
    other_kernel, partial = pl.pallas_call(
        lambda *refs: form(False, *refs),
        out_shape=(kernel_shape, shaped((samples, width), BF16)),
        compiler_params=ROOM,
        cost_estimate=cost,
        name="form_other",
    )(other, features, table, partial)

    arrivals = [partial] + [from_partner(partial, ROWS, flip) for flip in range(1, rows)]
    scale = 2.0 / total_blanks
    react_cost = pl.CostEstimate(
        flops=2 * held * width * samples,
        transcendentals=0,
        bytes_accessed=2 * held * (width + 2 * samples),
    )
    blank_current, weighted, reaction = pl.pallas_call(
        lambda *refs: weigh(scale, *refs),
        out_shape=(
            shaped((samples, blanks), BF16),
            shaped((samples, width), BF16),
            shaped(dense, BF16),
        ),
        compiler_params=ROOM,
        cost_estimate=react_cost,
        name="weigh",
    )(table, *arrivals, other_kernel)
    crossed = from_partner(reaction, "core", 1)
    reaction, blank_current = pl.pallas_call(
        lambda *refs: react(scale, *refs),
        out_shape=(shaped(dense, F32), shaped((samples, blanks), BF16)),
        compiler_params=ROOM,
        cost_estimate=react_cost,
        name="react",
    )(weighted, own_kernel, blank_current)
    pieces = (reaction + crossed.astype(F32)).astype(BF16)
    arrived = lax.all_to_all(pieces, COLS, 0, 0, tiled=True)
    coil_reaction = pl.pallas_call(
        finish,
        out_shape=shaped((coils, samples), F32),
        compiler_params=ROOM,
        name="finish",
    )(arrived)
    return (blank_current, coil_reaction.T)


def solution(mesh):
    split = Mesh(mesh.devices.reshape(SIZES), AXES)
    whole = P(None, AXES)
    return jax.shard_map(
        per_device,
        mesh=split,
        in_specs=(whole, P(AXES), whole, whole, P(AXES), P(AXES), P(), P()),
        out_specs=(whole, whole),
        check_vma=False,
    )
```

```python
import jax
import jax.numpy as jnp
from jax import lax
from jax.experimental import pallas as pl
from jax.experimental.pallas import tpu as pltpu
from jax.sharding import Mesh
from jax.sharding import PartitionSpec as P

AXES = ("zh", "zl", "xh", "y", "xl", "core")
SIZES = (4, 2, 2, 4, 2, 2)
ROWS = ("xh", "xl")
COLS = ("zl", "y", "zh")
LANES = 128
SUBLANES = 8
SLOT = 32
BF16 = jnp.bfloat16
F32 = jnp.float32
ROOM = pltpu.CompilerParams(vmem_limit_bytes=16 << 20)


def parts_of(value):
    high = value.astype(BF16).astype(F32)
    rest = value - high
    mid = rest.astype(BF16).astype(F32)
    low = (rest - mid).astype(BF16).astype(F32)
    return [high, mid, low]


def prepare(
    offset_ref,
    weight_ref,
    pos_ref,
    radius_ref,
    current_ref,
    blank_ref,
    rule_ref,
    cond_ref,
    payload_ref,
    tile_ref,
):
    coils, samples = current_ref.shape
    groups = coils // SUBLANES
    x, y, z = (pos_ref[pl.ds(axis, 1), :] for axis in range(3))
    radius = radius_ref[...]
    square = x * x + y * y + z * z + radius * radius
    rows = [part for value in (x, y, z, square) for part in parts_of(value)]
    count = len(rows)
    rows.append(jnp.zeros((16 - count, coils), F32))
    columns = jnp.concatenate(rows, 0).T
    geometry = [columns[SUBLANES * g : SUBLANES * (g + 1), :count] for g in range(groups)]
    geometry.append(jnp.zeros((SUBLANES, samples - count * groups), F32))
    geometry = jnp.concatenate(geometry, 1)
    current = current_ref[...].astype(F32)
    half = payload_ref.shape[1]
    left = current[:half]
    right = jnp.concatenate([current[half:], geometry], 0)
    payload = jnp.concatenate([left, right], 1).astype(BF16)
    for copy in range(payload_ref.shape[0]):
        payload_ref[copy] = payload
    points, rules = weight_ref.shape
    rule = rule_ref[...]
    rows = []
    for point in range(points):
        offsets = [jnp.zeros(rule.shape, F32) for _ in range(3)]
        weight = jnp.zeros(rule.shape, F32)
        for number in range(rules):
            here = rule == number
            for axis in range(3):
                offsets[axis] = jnp.where(here, offset_ref[axis, point, number], offsets[axis])
            weight = jnp.where(here, weight_ref[point, number], weight)
        rows += [blank_ref[pl.ds(axis, 1), :] + offsets[axis] for axis in range(3)]
        rows.append(weight)
    rows.append(cond_ref[...])
    rows.append(jnp.zeros((tile_ref.shape[0] - len(rows), rule.shape[1]), F32))
    tile_ref[...] = jnp.concatenate(rows, 0)


def blank_features(points, *refs):
    tiles, (feature_ref, row_ref) = refs[:-2], refs[-2:]
    whole = jnp.concatenate([tile[...] for tile in tiles], 1)
    width = whole.shape[1]
    for point in range(points):
        place = [whole[4 * point + axis : 4 * point + axis + 1] for axis in range(3)]
        square = place[0] * place[0] + place[1] * place[1] + place[2] * place[2]
        parts = [parts_of(value) for value in place]
        rows = []
        for level in range(3):
            for axis in range(3):
                rows += [-2.0 * parts[axis][level]] * 3
            rows += [jnp.full((1, width), 1.0 if level == 0 else 0.0, F32)] * 3
            rows.append(jnp.zeros((SLOT - 12, width), F32))
        rows += parts_of(square)
        rows.append(jnp.zeros((SLOT - 3, width), F32))
        feature_ref[point] = jnp.concatenate(rows, 0).astype(BF16)
    row_ref[...] = whole


def group_rows(payload, group):
    at = SUBLANES * (group % 3)
    rows = payload[:, at : at + SUBLANES, :]
    return rows.reshape(rows.shape[0] * SUBLANES, LANES)


def coil_features(geometry, group):
    lane = lax.broadcasted_iota(jnp.int32, geometry.shape, 1)
    at = LANES // 2 + 12 * group
    copies = [pltpu.roll(geometry, (SLOT * slot - at) % LANES, 1) for slot in range(3)]
    out = jnp.where(lane < SLOT, copies[0], jnp.where(lane < 2 * SLOT, copies[1], copies[2]))
    return jnp.where(lane < 3 * SLOT, out, 1.0).astype(BF16)


def form(first, payload_ref, feature_ref, row_ref, *refs):
    if first:
        kernel_ref, out_ref = refs
    else:
        before_ref, kernel_ref, out_ref = refs
    samples = out_ref.shape[0]
    points = feature_ref.shape[0]
    groups = kernel_ref.shape[0]
    payload = payload_ref[...]
    geometry = group_rows(payload, 2).astype(F32)
    for group in range(groups):
        coils = coil_features(geometry, group)
        block = None
        for point in range(points):
            squared = jnp.dot(coils, feature_ref[point], preferred_element_type=F32)
            term = row_ref[pl.ds(4 * point + 3, 1), :] * lax.rsqrt(squared)
            block = term if block is None else block + term
        kernel_ref[group] = block.astype(BF16)
    turned = [group_rows(payload, group).T for group in range(3)]
    current = [
        turned[group % 3][:samples] if group < 3 else turned[group % 3][samples:]
        for group in range(groups)
    ]
    kernel = kernel_ref[...].reshape(groups * kernel_ref.shape[1], kernel_ref.shape[2])
    total = jnp.dot(jnp.concatenate(current, 1), kernel, preferred_element_type=F32)
    if not first:
        total = total + before_ref[...]
    out_ref[...] = total.astype(out_ref.dtype)


def contract(kernel_ref, weighted):
    groups = kernel_ref.shape[0]
    twice = jnp.concatenate([weighted, weighted], 0)
    whole = [
        lax.dot_general(
            kernel_ref[group], twice, (((1,), (1,)), ((), ())), preferred_element_type=F32
        )
        for group in range(groups)
    ]
    shards = whole[0].shape[0] // SUBLANES
    whole = [part.reshape(shards, SUBLANES, LANES) for part in whole]
    lane = lax.broadcasted_iota(jnp.int32, whole[0].shape, 2)
    others = [whole[3], whole[4], pltpu.roll(whole[2], SUBLANES // 2, 1)]
    return [jnp.where(lane < LANES // 2, whole[group], others[group]) for group in range(3)]


def store_rows(out_ref, groups):
    for pair in range(out_ref.shape[2] // LANES):
        at = 2 * (pair % 4)
        rows = groups[pair // 4][:, at : at + 2, :]
        out_ref[:, :, pl.ds(pair * LANES, LANES)] = rows.astype(out_ref.dtype)


def weigh(scale, row_ref, *refs):
    arrivals = refs[:-4]
    kernel_ref, current_ref, weighted_ref, out_ref = refs[-4:]
    count = len(arrivals)
    width = current_ref.shape[1]
    blocks = []
    for block in range(count):
        total = None
        for flip in range(count):
            piece = arrivals[flip][:, pl.ds((block ^ flip) * width, width)].astype(F32)
            total = piece if total is None else total + piece
        blocks.append(total.astype(BF16))
    current_ref[...] = blocks[0]
    current = jnp.concatenate(blocks, 1).astype(F32)
    weighted = (row_ref[pl.ds(8, 1), :] * current).astype(BF16)
    weighted_ref[...] = weighted
    store_rows(out_ref, [scale * part for part in contract(kernel_ref, weighted)])


def react(scale, weighted_ref, kernel_ref, current_ref, out_ref, blank_ref):
    store_rows(out_ref, [scale * part for part in contract(kernel_ref, weighted_ref[...])])
    blank_ref[...] = current_ref[...]


def finish(arrived_ref, out_ref):
    parts = [arrived_ref[piece].astype(F32) for piece in range(arrived_ref.shape[0])]
    while len(parts) > 1:
        odd = parts[len(parts) // 2 * 2 :]
        parts = [a + b for a, b in zip(parts[::2], parts[1::2], strict=False)] + odd
    total = parts[0]
    rows = [total[:, LANES * pair : LANES * (pair + 1)] for pair in range(total.shape[1] // LANES)]
    rows = jnp.concatenate(rows, 0)
    samples = out_ref.shape[1]
    out_ref[...] = jnp.concatenate(
        [rows[:, :samples], rows[16:, samples:], rows[:16, samples:]], 0
    )


def from_partner(value, axis, flip):
    size = lax.axis_size(axis)
    return lax.ppermute(value, axis, [(i, i ^ flip) for i in range(size)])


def shaped(shape, dtype):
    return jax.ShapeDtypeStruct(shape, dtype)


def per_device(
    coil_pos, coil_radius, coil_current, blank_pos, blank_rule, blank_cond, quad_offset, quad_weight
):
    samples, coils = coil_current.shape
    blanks = blank_pos.shape[1]
    total_blanks = blanks * lax.axis_size(AXES)
    cols = lax.axis_size(COLS)
    rows = lax.axis_size(ROWS)
    points = quad_weight.shape[1]
    width = rows * blanks
    packed = (cols, 24, LANES)
    dense = (cols, 2, coils * samples // 2)
    kernel_shape = shaped((coils // SUBLANES, cols * SUBLANES, width), BF16)
    smem = pl.BlockSpec(memory_space=pltpu.SMEM)
    vmem = pl.BlockSpec(memory_space=pltpu.VMEM)

    arguments = (
        quad_offset.transpose(0, 2, 1),
        quad_weight.T,
        coil_pos,
        coil_radius[None, :],
        coil_current.T,
        blank_pos,
        blank_rule[None, :],
        blank_cond[None, :],
    )
    payload, tile = pl.pallas_call(
        prepare,
        out_shape=(shaped(packed, BF16), shaped((16, blanks), F32)),
        in_specs=[smem, smem] + [vmem] * 6,
        compiler_params=ROOM,
        name="prepare",
    )(*(pltpu.with_memory_space_constraint(value, pltpu.HBM) for value in arguments))
    own = lax.all_to_all(payload, COLS, 0, 0, tiled=True)
    tiles = [tile] + [from_partner(tile, ROWS, flip) for flip in range(1, rows)]
    features, table = pl.pallas_call(
        lambda *refs: blank_features(points, *refs),
        out_shape=(shaped((points, LANES, width), BF16), shaped((16, width), F32)),
        compiler_params=ROOM,
        name="blank_features",
    )(*tiles)
    own, features, table = lax.optimization_barrier((own, features, table))
    other = from_partner(own, "core", 1)
    held = cols * coils
    cost = pl.CostEstimate(
        flops=2 * held * width * LANES * (points + 1),
        transcendentals=points * held * width,
        bytes_accessed=2 * held * (width + LANES),
    )
    own_kernel, partial = pl.pallas_call(
        lambda *refs: form(True, *refs),
        out_shape=(kernel_shape, shaped((samples, width), F32)),
        compiler_params=ROOM,
        cost_estimate=cost,
        name="form_own",
    )(own, features, table)
    other_kernel, partial = pl.pallas_call(
        lambda *refs: form(False, *refs),
        out_shape=(kernel_shape, shaped((samples, width), BF16)),
        compiler_params=ROOM,
        cost_estimate=cost,
        name="form_other",
    )(other, features, table, partial)

    arrivals = [partial] + [from_partner(partial, ROWS, flip) for flip in range(1, rows)]
    scale = 2.0 / total_blanks
    react_cost = pl.CostEstimate(
        flops=2 * held * width * samples,
        transcendentals=0,
        bytes_accessed=2 * held * (width + 2 * samples),
    )
    blank_current, weighted, reaction = pl.pallas_call(
        lambda *refs: weigh(scale, *refs),
        out_shape=(
            shaped((samples, blanks), BF16),
            shaped((samples, width), BF16),
            shaped(dense, BF16),
        ),
        compiler_params=ROOM,
        cost_estimate=react_cost,
        name="weigh",
    )(table, *arrivals, other_kernel)
    crossed = from_partner(reaction, "core", 1)
    reaction, blank_current = pl.pallas_call(
        lambda *refs: react(scale, *refs),
        out_shape=(shaped(dense, F32), shaped((samples, blanks), BF16)),
        compiler_params=ROOM,
        cost_estimate=react_cost,
        name="react",
    )(weighted, own_kernel, blank_current)
    pieces = (reaction + crossed.astype(F32)).astype(BF16)
    arrived = lax.all_to_all(pieces, COLS, 0, 0, tiled=True)
    coil_reaction = pl.pallas_call(
        finish,
        out_shape=shaped((coils, samples), F32),
        compiler_params=ROOM,
        name="finish",
    )(arrived)
    return (blank_current, coil_reaction.T)


def solution(mesh):
    split = Mesh(mesh.devices.reshape(SIZES), AXES)
    whole = P(None, AXES)
    return jax.shard_map(
        per_device,
        mesh=split,
        in_specs=(whole, P(AXES), whole, whole, P(AXES), P(AXES), P(), P()),
        out_specs=(whole, whole),
        check_vma=False,
    )
```

```python
import jax
import jax.numpy as jnp
from jax import lax
from jax.experimental import pallas as pl
from jax.experimental.pallas import tpu as pltpu
from jax.sharding import Mesh
from jax.sharding import PartitionSpec as P

AXES = ("zh", "zl", "xh", "y", "xl", "core")
SIZES = (4, 2, 2, 4, 2, 2)
ROWS = ("xh", "xl")
COLS = ("zl", "y", "zh")
LANES = 128
SUBLANES = 8
SLOT = 32
BF16 = jnp.bfloat16
F32 = jnp.float32
ROOM = pltpu.CompilerParams(vmem_limit_bytes=16 << 20)


def parts_of(value):
    high = value.astype(BF16).astype(F32)
    rest = value - high
    mid = rest.astype(BF16).astype(F32)
    low = (rest - mid).astype(BF16).astype(F32)
    return [high, mid, low]


def prepare(
    offset_ref,
    weight_ref,
    pos_ref,
    radius_ref,
    current_ref,
    blank_ref,
    rule_ref,
    cond_ref,
    payload_ref,
    tile_ref,
):
    coils, samples = current_ref.shape
    groups = coils // SUBLANES
    x, y, z = (pos_ref[pl.ds(axis, 1), :] for axis in range(3))
    radius = radius_ref[...]
    square = x * x + y * y + z * z + radius * radius
    rows = [part for value in (x, y, z, square) for part in parts_of(value)]
    count = len(rows)
    rows.append(jnp.zeros((16 - count, coils), F32))
    columns = jnp.concatenate(rows, 0).T
    geometry = [columns[SUBLANES * g : SUBLANES * (g + 1), :count] for g in range(groups)]
    geometry.append(jnp.zeros((SUBLANES, samples - count * groups), F32))
    geometry = jnp.concatenate(geometry, 1)
    current = current_ref[...].astype(F32)
    half = payload_ref.shape[1]
    left = current[:half]
    right = jnp.concatenate([current[half:], geometry], 0)
    payload = jnp.concatenate([left, right], 1).astype(BF16)
    for copy in range(payload_ref.shape[0]):
        payload_ref[copy] = payload
    points, rules = weight_ref.shape
    rule = rule_ref[...]
    rows = []
    for point in range(points):
        offsets = [jnp.zeros(rule.shape, F32) for _ in range(3)]
        weight = jnp.zeros(rule.shape, F32)
        for number in range(rules):
            here = rule == number
            for axis in range(3):
                offsets[axis] = jnp.where(here, offset_ref[axis, point, number], offsets[axis])
            weight = jnp.where(here, weight_ref[point, number], weight)
        rows += [blank_ref[pl.ds(axis, 1), :] + offsets[axis] for axis in range(3)]
        rows.append(weight)
    rows.append(cond_ref[...])
    rows.append(jnp.zeros((tile_ref.shape[0] - len(rows), rule.shape[1]), F32))
    tile_ref[...] = jnp.concatenate(rows, 0)


def blank_features(points, *refs):
    tiles, (feature_ref, row_ref) = refs[:-2], refs[-2:]
    whole = jnp.concatenate([tile[...] for tile in tiles], 1)
    width = whole.shape[1]
    for point in range(points):
        place = [whole[4 * point + axis : 4 * point + axis + 1] for axis in range(3)]
        square = place[0] * place[0] + place[1] * place[1] + place[2] * place[2]
        parts = [parts_of(value) for value in place]
        rows = []
        for level in range(3):
            for axis in range(3):
                rows += [-2.0 * parts[axis][level]] * 3
            rows += [jnp.full((1, width), 1.0 if level == 0 else 0.0, F32)] * 3
            rows.append(jnp.zeros((SLOT - 12, width), F32))
        rows += parts_of(square)
        rows.append(jnp.zeros((SLOT - 3, width), F32))
        feature_ref[point] = jnp.concatenate(rows, 0).astype(BF16)
    row_ref[...] = whole


def group_rows(payload, group):
    at = SUBLANES * (group % 3)
    rows = payload[:, at : at + SUBLANES, :]
    return rows.reshape(rows.shape[0] * SUBLANES, LANES)


def coil_features(geometry, group):
    lane = lax.broadcasted_iota(jnp.int32, geometry.shape, 1)
    at = LANES // 2 + 12 * group
    copies = [pltpu.roll(geometry, (SLOT * slot - at) % LANES, 1) for slot in range(3)]
    out = jnp.where(lane < SLOT, copies[0], jnp.where(lane < 2 * SLOT, copies[1], copies[2]))
    return jnp.where(lane < 3 * SLOT, out, 1.0).astype(BF16)


def form(first, payload_ref, feature_ref, row_ref, *refs):
    if first:
        kernel_ref, out_ref = refs
    else:
        before_ref, kernel_ref, out_ref = refs
    samples = out_ref.shape[0]
    points = feature_ref.shape[0]
    groups = kernel_ref.shape[0]
    payload = payload_ref[...]
    geometry = group_rows(payload, 2).astype(F32)
    for group in range(groups):
        coils = coil_features(geometry, group)
        block = None
        for point in range(points):
            squared = jnp.dot(coils, feature_ref[point], preferred_element_type=F32)
            term = row_ref[pl.ds(4 * point + 3, 1), :] * lax.rsqrt(squared)
            block = term if block is None else block + term
        kernel_ref[group] = block.astype(BF16)
    turned = [group_rows(payload, group).T for group in range(3)]
    current = [
        turned[group % 3][:samples] if group < 3 else turned[group % 3][samples:]
        for group in range(groups)
    ]
    kernel = kernel_ref[...].reshape(groups * kernel_ref.shape[1], kernel_ref.shape[2])
    total = jnp.dot(jnp.concatenate(current, 1), kernel, preferred_element_type=F32)
    if not first:
        total = total + before_ref[...]
    out_ref[...] = total.astype(out_ref.dtype)


def contract(kernel_ref, weighted):
    groups = kernel_ref.shape[0]
    twice = jnp.concatenate([weighted, weighted], 0)
    whole = [
        lax.dot_general(
            kernel_ref[group], twice, (((1,), (1,)), ((), ())), preferred_element_type=F32
        )
        for group in range(groups)
    ]
    shards = whole[0].shape[0] // SUBLANES
    whole = [part.reshape(shards, SUBLANES, LANES) for part in whole]
    lane = lax.broadcasted_iota(jnp.int32, whole[0].shape, 2)
    others = [whole[3], whole[4], pltpu.roll(whole[2], SUBLANES // 2, 1)]
    return [jnp.where(lane < LANES // 2, whole[group], others[group]) for group in range(3)]


def store_rows(out_ref, groups):
    for pair in range(out_ref.shape[2] // LANES):
        at = 2 * (pair % 4)
        rows = groups[pair // 4][:, at : at + 2, :]
        out_ref[:, :, pl.ds(pair * LANES, LANES)] = rows.astype(out_ref.dtype)


def weigh(scale, row_ref, *refs):
    arrivals = refs[:-4]
    kernel_ref, current_ref, weighted_ref, out_ref = refs[-4:]
    count = len(arrivals)
    width = current_ref.shape[1]
    blocks = []
    for block in range(count):
        total = None
        for flip in range(count):
            piece = arrivals[flip][:, pl.ds((block ^ flip) * width, width)].astype(F32)
            total = piece if total is None else total + piece
        blocks.append(total.astype(BF16))
    current_ref[...] = blocks[0]
    current = jnp.concatenate(blocks, 1).astype(F32)
    weighted = (row_ref[pl.ds(8, 1), :] * current).astype(BF16)
    weighted_ref[...] = weighted
    store_rows(out_ref, [scale * part for part in contract(kernel_ref, weighted)])


def react(scale, weighted_ref, kernel_ref, out_ref):
    store_rows(out_ref, [scale * part for part in contract(kernel_ref, weighted_ref[...])])


def finish(arrived_ref, current_ref, out_ref, blank_ref):
    blank_ref[...] = current_ref[...]
    parts = [arrived_ref[piece].astype(F32) for piece in range(arrived_ref.shape[0])]
    while len(parts) > 1:
        odd = parts[len(parts) // 2 * 2 :]
        parts = [a + b for a, b in zip(parts[::2], parts[1::2], strict=False)] + odd
    total = parts[0]
    rows = [total[:, LANES * pair : LANES * (pair + 1)] for pair in range(total.shape[1] // LANES)]
    rows = jnp.concatenate(rows, 0)
    samples = out_ref.shape[1]
    out_ref[...] = jnp.concatenate(
        [rows[:, :samples], rows[16:, samples:], rows[:16, samples:]], 0
    )


def from_partner(value, axis, flip):
    size = lax.axis_size(axis)
    return lax.ppermute(value, axis, [(i, i ^ flip) for i in range(size)])


def shaped(shape, dtype):
    return jax.ShapeDtypeStruct(shape, dtype)


def per_device(
    coil_pos, coil_radius, coil_current, blank_pos, blank_rule, blank_cond, quad_offset, quad_weight
):
    samples, coils = coil_current.shape
    blanks = blank_pos.shape[1]
    total_blanks = blanks * lax.axis_size(AXES)
    cols = lax.axis_size(COLS)
    rows = lax.axis_size(ROWS)
    points = quad_weight.shape[1]
    width = rows * blanks
    packed = (cols, 24, LANES)
    dense = (cols, 2, coils * samples // 2)
    kernel_shape = shaped((coils // SUBLANES, cols * SUBLANES, width), BF16)
    smem = pl.BlockSpec(memory_space=pltpu.SMEM)
    vmem = pl.BlockSpec(memory_space=pltpu.VMEM)

    arguments = (
        quad_offset.transpose(0, 2, 1),
        quad_weight.T,
        coil_pos,
        coil_radius[None, :],
        coil_current.T,
        blank_pos,
        blank_rule[None, :],
        blank_cond[None, :],
    )
    payload, tile = pl.pallas_call(
        prepare,
        out_shape=(shaped(packed, BF16), shaped((16, blanks), F32)),
        in_specs=[smem, smem] + [vmem] * 6,
        compiler_params=ROOM,
        name="prepare",
    )(*(pltpu.with_memory_space_constraint(value, pltpu.HBM) for value in arguments))
    own = lax.all_to_all(payload, COLS, 0, 0, tiled=True)
    tiles = [tile] + [from_partner(tile, ROWS, flip) for flip in range(1, rows)]
    features, table = pl.pallas_call(
        lambda *refs: blank_features(points, *refs),
        out_shape=(shaped((points, LANES, width), BF16), shaped((16, width), F32)),
        compiler_params=ROOM,
        name="blank_features",
    )(*tiles)
    own, features, table = lax.optimization_barrier((own, features, table))
    other = from_partner(own, "core", 1)
    held = cols * coils
    cost = pl.CostEstimate(
        flops=2 * held * width * LANES * (points + 1),
        transcendentals=points * held * width,
        bytes_accessed=2 * held * (width + LANES),
    )
    own_kernel, partial = pl.pallas_call(
        lambda *refs: form(True, *refs),
        out_shape=(kernel_shape, shaped((samples, width), F32)),
        compiler_params=ROOM,
        cost_estimate=cost,
        name="form_own",
    )(own, features, table)
    other_kernel, partial = pl.pallas_call(
        lambda *refs: form(False, *refs),
        out_shape=(kernel_shape, shaped((samples, width), BF16)),
        compiler_params=ROOM,
        cost_estimate=cost,
        name="form_other",
    )(other, features, table, partial)

    arrivals = [partial] + [from_partner(partial, ROWS, flip) for flip in range(1, rows)]
    scale = 2.0 / total_blanks
    react_cost = pl.CostEstimate(
        flops=2 * held * width * samples,
        transcendentals=0,
        bytes_accessed=2 * held * (width + 2 * samples),
    )
    blank_current, weighted, reaction = pl.pallas_call(
        lambda *refs: weigh(scale, *refs),
        out_shape=(
            shaped((samples, blanks), BF16),
            shaped((samples, width), BF16),
            shaped(dense, BF16),
        ),
        compiler_params=ROOM,
        cost_estimate=react_cost,
        name="weigh",
    )(table, *arrivals, other_kernel)
    crossed = from_partner(reaction, "core", 1)
    reaction = pl.pallas_call(
        lambda *refs: react(scale, *refs),
        out_shape=shaped(dense, F32),
        compiler_params=ROOM,
        cost_estimate=react_cost,
        name="react",
    )(weighted, own_kernel)
    pieces = (reaction + crossed.astype(F32)).astype(BF16)
    arrived = lax.all_to_all(pieces, COLS, 0, 0, tiled=True)
    coil_reaction, blank_current = pl.pallas_call(
        finish,
        out_shape=(shaped((coils, samples), F32), shaped((samples, blanks), BF16)),
        compiler_params=ROOM,
        name="finish",
    )(arrived, blank_current)
    return (blank_current, coil_reaction.T)


def solution(mesh):
    split = Mesh(mesh.devices.reshape(SIZES), AXES)
    whole = P(None, AXES)
    return jax.shard_map(
        per_device,
        mesh=split,
        in_specs=(whole, P(AXES), whole, whole, P(AXES), P(AXES), P(), P()),
        out_specs=(whole, whole),
        check_vma=False,
    )
```
